256 devices in a mesh: leaf: 8 (over x, core), row: 32 (over y, z).
Axes of the slice: x: 4, y: 4, z: 8, core: 2. Of those that a mesh axis runs over, the one named last changes fastest.
Arguments:
- loc_rhs: float32 [8, 32, 512, 128], P('leaf', 'row'), may hold values from -6 to 6
- loc_inverse: float32 [8, 32, 512, 512], P('leaf', 'row'), may hold values from -0.25 to 0.25
- loc_coupling: float32 [8, 32, 512, 512], P('leaf', 'row'), may hold values from -0.09375 to 0.09375
- loc_pivots: float32 [8, 32, 512], P('leaf', 'row'), may hold values from 0.5 to 4
- pattern: int32 [8, 32, 4], P('leaf', 'row'), may hold values from 0 to 29, as said below
- win_rhs: float32 [4, 2048, 128], P(None, ('leaf', 'row')), may hold values from -6 to 6
- win_pivots: float32 [4, 2048], P(None, ('leaf', 'row')), may hold values from 0.5 to 4
- win_inverse: float32 [32, 120, 2048], P('row', None, 'leaf'), may hold values from -0.125 to 0.125
- win_coupling: float32 [32, 112, 2048], P('row', None, 'leaf'), may hold values from -0.125 to 0.125
Outputs:
- loc_solution: float32 [8, 32, 512, 128], P('leaf', 'row')
- win_solution: float32 [4, 2048, 128], P(None, ('leaf', 'row'))
The draws below stay inside these ranges and needn't reach their ends.
Inputs may be any that keep to these rules, and one draw needn't show every extreme that they name: `pattern`: on each device the 4 tile numbers are distinct; number p stands for rows p * 128 to (p + 1) * 128 - 1 of the path of the device's leaf index.
All inputs are finite; a program needn't handle non-finite values.
Results may differ from the reference program's by a relative error of at most 0.0001.
Values sent between devices are 32-bit elements; how exact they have to be, the bound alone decides.
A program may use at most 64 MiB of HBM per device.

```python
import math
import jax
import jax.numpy as jnp
from jax import lax

RHS = 128
BASE = 256
LOC = 512
TILE = 128
TILES = 4
LEAVES = 8
RANKS = 32
LEVELS = 4
PIECE = 8
PTILES = 30


def choose_tiles(single):
    return jax.random.permutation(single, PTILES)[:TILES]


def draw_pattern(key, part):
    subkeys = jax.random.split(key, LEAVES * RANKS)
    chosen = jax.vmap(choose_tiles)(subkeys)
    return chosen.reshape(LEAVES, RANKS, TILES).astype(jnp.int32)


def shard_levels(stream_key, dims, cuts, low, largest):
    factor_of, own = 1.0, jax.random.fold_in(stream_key, 6)
    for dim, blocks in cuts:
        draws = jnp.exp(jax.random.uniform(jax.random.fold_in(own, dim), (blocks,), jnp.float32, low / len(cuts), largest / len(cuts)))
        factor_of = factor_of * jnp.repeat(draws, dims[dim] // blocks).reshape([-1 if axis == dim else 1 for axis in range(len(dims))])
    return factor_of


def normal_values(stream_key, dims, width, reach, cuts=(), held_as=jnp.bfloat16):
    array = width * jax.random.normal(stream_key, dims, jnp.float32)
    if cuts:
        array = array * shard_levels(stream_key, dims, cuts, -0.22, 0.18)
    return jnp.clip(array, -reach, reach).astype(held_as)


def setup_inputs(seed: int = 0) -> dict:
    seeds = jax.random.split(jax.random.key(seed), 10)
    loc_rhs = normal_values(seeds[0], (LEAVES, RANKS, LOC, RHS), 1.0, 6.0, ((0, 8), (1, 32)), jnp.float32)
    loc_inverse = normal_values(seeds[1], (LEAVES, RANKS, LOC, LOC), LOC ** -0.5, 0.25, ((0, 8), (1, 32)), jnp.float32)
    loc_coupling = normal_values(seeds[2], (LEAVES, RANKS, TILES * TILE, LOC), (8 * LOC) ** -0.5, 0.09375, ((0, 8), (1, 32)), jnp.float32)
    loc_pivots = jnp.clip(jnp.exp(math.log(4.0) - 2.0794415 * jax.random.uniform(seeds[3], (LEAVES, RANKS, LOC), jnp.float32) ** shard_levels(seeds[3], (LEAVES, RANKS, LOC), ((0, 8), (1, 32)), -0.2, 0.2)), 0.5, 4.0)
    pattern = draw_pattern(jax.random.fold_in(seeds[9], 71), 0)
    win_rhs = normal_values(seeds[5], (LEVELS, LEAVES * BASE, RHS), 1.0, 6.0, ((1, 256),), jnp.float32)
    win_pivots = jnp.clip(jnp.exp(math.log(4.0) - 2.0794415 * jax.random.uniform(seeds[6], (LEVELS, LEAVES * BASE), jnp.float32) ** shard_levels(seeds[6], (LEVELS, LEAVES * BASE), ((1, 256),), -0.2, 0.2)), 0.5, 4.0)
    win_inverse = normal_values(seeds[7], (RANKS, (2 * LEAVES - 1) * PIECE, LEAVES * BASE), (LEAVES * BASE) ** -0.5, 0.125, ((0, 32), (2, 8)), jnp.float32)
    win_coupling = normal_values(seeds[8], (RANKS, (2 * LEAVES - 2) * PIECE, LEAVES * BASE), (LEAVES * BASE) ** -0.5, 0.125, ((0, 32), (2, 8)), jnp.float32)
    return {"loc_rhs": loc_rhs, "loc_inverse": loc_inverse, "loc_coupling": loc_coupling, "loc_pivots": loc_pivots, "pattern": pattern, "win_rhs": win_rhs, "win_pivots": win_pivots, "win_inverse": win_inverse, "win_coupling": win_coupling}


PRECISE = lax.Precision.HIGHEST


def strict_lower(matrix):
    extent = matrix.shape[-1]
    row_ids = jnp.arange(extent, dtype=jnp.int32)[:, None]
    col_ids = jnp.arange(extent, dtype=jnp.int32)[None, :]
    return jnp.where(col_ids < row_ids, matrix, jnp.zeros_like(matrix))


def level_rows(stacked, offset, group_span):
    chosen = stacked[:, offset:offset + group_span * PIECE, :]
    chosen = chosen.reshape(RANKS, group_span, PIECE, LEAVES * BASE)
    chosen = jnp.transpose(chosen, (1, 0, 2, 3))
    return chosen.reshape(group_span * BASE, LEAVES * BASE)


def node_blocks(matrix):
    node_width = matrix.shape[0]
    node_count = matrix.shape[1] // node_width
    return jnp.transpose(matrix.reshape(node_width, node_count, node_width), (1, 0, 2))


def local_forward(operands):
    right_side, inverse, coupling = operands
    solved = right_side + jnp.dot(strict_lower(inverse), right_side, precision=PRECISE)
    return solved, jnp.dot(coupling, solved, precision=PRECISE)


def local_backward(operands):
    scaled, inverse, coupling, picked = operands
    remainder = scaled - jnp.dot(coupling.T, picked, precision=PRECISE)
    return remainder + jnp.dot(strict_lower(inverse).T, remainder, precision=PRECISE)


def reference(loc_rhs, loc_inverse, loc_coupling, loc_pivots, pattern, win_rhs, win_pivots, win_inverse, win_coupling):
    devices = LEAVES * RANKS
    inverses = loc_inverse.reshape(devices, LOC, LOC)
    couplings = loc_coupling.reshape(devices, TILES * TILE, LOC)
    solved_loc, loc_terms = lax.map(local_forward, (loc_rhs.reshape(devices, LOC, RHS), inverses, couplings))
    leaf_ids = jnp.broadcast_to(jnp.arange(LEAVES, dtype=jnp.int32)[:, None, None], (LEAVES, RANKS, TILES))
    path_rows = jnp.zeros((LEAVES, PTILES, TILE, RHS), jnp.float32)
    path_rows = path_rows.at[leaf_ids, pattern].add(loc_terms.reshape(LEAVES, RANKS, TILES, TILE, RHS))
    path_rows = path_rows.reshape(LEAVES, PTILES * TILE, RHS)
    diagonals = []
    links = []
    local_sums = []
    for height in range(LEVELS):
        group_span = 2 ** height
        node_width = BASE * group_span
        diagonals.append(strict_lower(node_blocks(level_rows(win_inverse, (group_span - 1) * PIECE, group_span))))
        if height + 1 < LEVELS:
            links.append(node_blocks(level_rows(win_coupling, (2 * group_span - 2) * PIECE, 2 * group_span)))
        segment = path_rows[:, BASE * (group_span - 1):BASE * (2 * group_span - 1)]
        segment = segment.reshape(LEAVES // group_span, group_span, node_width, RHS).sum(axis=1)
        local_sums.append(segment.reshape(LEAVES * BASE, RHS))
    from_children = jnp.zeros((LEAVES * BASE, RHS), jnp.float32)
    solved = []
    for height in range(LEVELS):
        node_width = BASE * 2 ** height
        residual = (win_rhs[height] - local_sums[height] - from_children).reshape(-1, node_width, RHS)
        current = residual + jnp.einsum("kab,kbx->kax", diagonals[height], residual, precision=PRECISE)
        solved.append(current.reshape(LEAVES * BASE, RHS))
        if height + 1 < LEVELS:
            stacked = current.reshape(-1, 2 * node_width, RHS)
            from_children = jnp.einsum("kab,kbx->kax", links[height], stacked, precision=PRECISE).reshape(LEAVES * BASE, RHS)
    from_parent = jnp.zeros((LEAVES * BASE, RHS), jnp.float32)
    results = [None] * LEVELS
    for height in reversed(range(LEVELS)):
        node_width = BASE * 2 ** height
        wanted = (solved[height] / win_pivots[height][:, None] - from_parent).reshape(-1, node_width, RHS)
        current = wanted + jnp.einsum("kba,kbx->kax", diagonals[height], wanted, precision=PRECISE)
        results[height] = current.reshape(LEAVES * BASE, RHS)
        if height > 0:
            from_parent = jnp.einsum("kba,kbx->kax", links[height - 1], current, precision=PRECISE).reshape(LEAVES * BASE, RHS)
    pieces = []
    for height in range(LEVELS):
        group_span = 2 ** height
        node_vecs = results[height].reshape(LEAVES // group_span, BASE * group_span, RHS)
        pieces.append(jnp.repeat(node_vecs, group_span, axis=0))
    full_path = jnp.concatenate(pieces, axis=1).reshape(LEAVES, PTILES, TILE, RHS)
    picked = full_path[leaf_ids, pattern].reshape(devices, TILES * TILE, RHS)
    scaled_loc = solved_loc / loc_pivots.reshape(devices, LOC)[:, :, None]
    answer = lax.map(local_backward, (scaled_loc, inverses, couplings, picked))
    return answer.reshape(LEAVES, RANKS, LOC, RHS), jnp.stack(results)
```

```python
import functools

import jax
import jax.numpy as jnp
from jax import lax
from jax.experimental import pallas as pl
from jax.experimental.pallas import tpu as pltpu
from jax.sharding import PartitionSpec as P

MESH = pl.DeviceIdType.MESH
F32 = jnp.float32
BF16 = jnp.bfloat16
NB, NY, NZ, NA, LEVELS = 32, 4, 8, 8, 4


def split(x):
    hi = x.astype(BF16)
    return hi, (x - hi.astype(F32)).astype(BF16)


def mm(left, right, dims=(((1,), (0,)), ((), ()))):
    return lax.dot_general(left, right, dims, preferred_element_type=F32)


def dot3(left, right):
    (lh, ll), (rh, rl) = left, right
    return mm(lh, rh) + (mm(lh, rl) + mm(ll, rh))


def flip(a, d):
    out = a
    for k in range(3):
        if (d >> k) & 1:
            out = out + (1 << k) * (1 - 2 * lax.rem(lax.div(a, 1 << k), 2))
    return out


def at8(value):
    return pl.multiple_of(value, 8)


TOP = [(2**l - 1) * 8 for l in range(LEVELS)]
LINK = [(2 * 2**l - 2) * 8 for l in range(LEVELS)]
SLOT = [0, 0, 1, 4]

PAT, TERM, USUM, PICK = 0, 1, 2, 3
AZ, AY, LU, AG, PX, YX, ZX, XX, RS, PY, BX = 4, 7, 10, 14, 18, 22, 26, 30, 34, 38, 42
NSEM = 46


def kernel(rhs, inv, cpl, piv, pat, wrhs, wpiv, winv, wcpl, out_loc, out_win,
           st_h, st_l, ct_h, ct_l, yloc, zloc, patrecv, sel, tsend, trecv, usend, urecv, ubuf, lurecv,
           strict, aall, bpeer, mbuf, gath, part, precv, yrecv, zbuf, xbuf,
           rsend, rrecv, xpath, psend, precv2, send, recv):
    a = lax.axis_index("leaf")
    b = lax.axis_index("row")
    y = lax.div(b, NZ)
    z = lax.rem(b, NZ)
    own8 = at8(b * 8)

    barrier = pltpu.get_barrier_semaphore()

    def greet(d, carry):
        pl.semaphore_signal(barrier, inc=1, device_id=(a, lax.rem(b + d, NB)), device_id_type=MESH)
        return carry

    lax.fori_loop(1, NB, greet, 0)
    for d in range(1, NA):
        pl.semaphore_signal(barrier, inc=1, device_id=(flip(a, d), b), device_id_type=MESH)

    def push(src, dst, sem, leaf, row):
        pltpu.make_async_remote_copy(
            src_ref=src, dst_ref=dst, send_sem=send.at[sem], recv_sem=recv.at[sem],
            device_id=(leaf, row), device_id_type=MESH,
        ).start()

    def done(which, sem, view):
        pltpu.make_async_copy(view, view, which.at[sem]).wait()

    def zpeers(body):
        def step(d, carry):
            z2 = lax.rem(z + d, NZ)
            body(z2, y * NZ + z2)
            return carry

        lax.fori_loop(1, NZ, step, 0)

    def ypeers(body):
        def step(d, carry):
            body(lax.rem(b + d * NZ, NB))
            return carry

        lax.fori_loop(1, NY, step, 0)

    def rowpeers(body):
        def step(d, carry):
            body(lax.rem(b + d, NB))
            return carry

        lax.fori_loop(1, NB, step, 0)

    for l in range(LEVELS):
        n = 2**l * 8
        rows = lax.broadcasted_iota(jnp.int32, (n, 256), 0)
        cols = lax.broadcasted_iota(jnp.int32, (n, 256), 1)
        row_id = lax.div(rows, 8) * 256 + b * 8 + lax.rem(rows, 8)
        col_id = lax.rem(a, 2**l) * 256 + cols
        block = jnp.where(col_id < row_id, winv[TOP[l] : TOP[l] + n, :], 0.0)
        strict[TOP[l] : TOP[l] + n, :] = block
        if l < 3:
            for q in range(2**l):
                aall[2**l - 1 + q, b] = block[8 * q : 8 * q + 8]
    strict[120:128, :] = jnp.zeros((8, 256), F32)

    lane = lax.broadcasted_iota(jnp.int32, (1, 128), 1)
    for t in range(4):
        tile = pat[0, t]
        mark = lax.rem(tile, 2) * 16 + lax.div(tile, 2)
        patrecv[z, t : t + 1, :] = jnp.where(lane == mark, 1.0, 0.0).astype(F32)

    low_row = lax.broadcasted_iota(jnp.int32, (128, 128), 0)
    low_col = lax.broadcasted_iota(jnp.int32, (128, 128), 1)
    low = low_col < low_row
    right = split(rhs[...])
    for r in range(4):
        acc = rhs[128 * r : 128 * r + 128, :]
        diag = jnp.where(low, inv[128 * r : 128 * r + 128, 128 * r : 128 * r + 128], 0.0)
        acc = acc + dot3(split(diag), (right[0][128 * r : 128 * r + 128], right[1][128 * r : 128 * r + 128]))
        if r:
            acc = acc + dot3(split(inv[128 * r : 128 * r + 128, : 128 * r]), (right[0][: 128 * r], right[1][: 128 * r]))
        yloc[128 * r : 128 * r + 128, :] = acc

    pl.semaphore_wait(barrier, NB - 1 + NA - 1)

    zpeers(lambda z2, row: push(patrecv.at[z], patrecv.at[z], PAT, a, row))
    zpeers(lambda z2, row: push(aall.at[pl.ds(0, 1), b], aall.at[pl.ds(0, 1), b], AZ, a, row))

    solved = split(yloc[...])
    for t in range(4):
        term = dot3(split(cpl[128 * t : 128 * t + 128, :]), solved)
        for i in range(16):
            ih, z2 = divmod(i, 8)
            at = z2 * 64 + t * 16 + ih * 8
            tsend[at : at + 8, :] = term[8 * i : 8 * i + 8]
    own64 = at8(z * 64)
    trecv[pl.ds(own64, 64), :] = tsend[pl.ds(own64, 64), :]
    zpeers(lambda z2, row: push(tsend.at[pl.ds(at8(z2 * 64), 64)], trecv.at[pl.ds(own64, 64)], TERM, a, row))

    for l in (1, 2):
        n = 2**l
        zpeers(lambda z2, row: push(aall.at[pl.ds(n - 1, n), b], aall.at[pl.ds(n - 1, n), b], AZ + l, a, row))
    for d in range(1, 4):
        first = 16 if d == 1 else 48
        push(wcpl.at[pl.ds(first, 112 - first)], bpeer.at[pl.ds(96 * (d - 1) + first - 16, 112 - first)], BX + d, flip(a, d), b)

    def forward_a(l):
        n = 2**l
        done(recv, AZ + l, aall.at[pl.ds(0, n), pl.ds(0, 7)])
        slab = aall.at[pl.ds(n - 1, n), pl.ds(y * NZ, NZ)]
        ypeers(lambda row: push(slab, slab, AY + l, a, row))

    forward_a(0)

    sel[...] = jnp.zeros((128, 128), F32)
    xpath[...] = jnp.zeros((512, 128), F32)
    for r in range(4):
        for c in range(4):
            blk = cpl[128 * r : 128 * r + 128, 128 * c : 128 * c + 128].T
            h, lo = split(blk)
            ct_h[128 * c : 128 * c + 128, 128 * r : 128 * r + 128] = h
            ct_l[128 * c : 128 * c + 128, 128 * r : 128 * r + 128] = lo
            if c <= r:
                blk = inv[128 * r : 128 * r + 128, 128 * c : 128 * c + 128]
                if c == r:
                    blk = jnp.where(low, blk, 0.0)
                h, lo = split(blk.T)
                st_h[128 * c : 128 * c + 128, 128 * r : 128 * r + 128] = h
                st_l[128 * c : 128 * c + 128, 128 * r : 128 * r + 128] = lo
    strict_t = jnp.concatenate([strict[:, :128].T, strict[:, 128:].T], axis=0)
    strict_t = split(strict_t)
    wide = jnp.broadcast_to(piv[...], (128, 512))
    for r in range(4):
        zloc[128 * r : 128 * r + 128, :] = yloc[128 * r : 128 * r + 128, :] / wide[:, 128 * r : 128 * r + 128].T

    done(recv, PAT, patrecv.at[pl.ds(0, 7)])
    for s in range(8):
        sel[4 * s : 4 * s + 4, :] = patrecv[s]
    chosen_t = sel[...].T[:32, :32].astype(BF16)
    done(recv, TERM, trecv.at[pl.ds(0, 448)])
    cols = split(jnp.concatenate([trecv[pl.ds(j, 32, stride=16), :] for j in range(16)], axis=1))
    placed = mm(chosen_t, cols[0]) + mm(chosen_t, cols[1])
    for j in range(16):
        ih, i8 = divmod(j, 8)
        for h in range(2):
            usend[pl.ds(128 * (2 * h + ih) + i8, 16, stride=8), :] = placed[16 * h : 16 * h + 16, 128 * j : 128 * j + 128]
    own128 = at8(y * 128)
    urecv[pl.ds(own128, 128), :] = usend[pl.ds(own128, 128), :]
    ypeers(lambda row: push(usend.at[pl.ds(at8(lax.div(row, NZ) * 128), 128)], urecv.at[pl.ds(own128, 128)], USUM, a, row))

    forward_a(1)
    done(recv, AY, aall.at[pl.ds(0, 1), pl.ds(0, 24)])
    mbuf[0:16, :] = wcpl[0:16, :] + dot3(split(wcpl[0:16, :]), split(aall[0].reshape(256, 256)))
    forward_a(2)

    done(recv, USUM, urecv.at[pl.ds(0, 384)])
    ubuf[...] = (urecv[0:128, :] + urecv[128:256, :]) + (urecv[256:384, :] + urecv[384:512, :])
    for l in range(1, LEVELS):
        for d in range(1, 2**l):
            at = at8(TOP[l] + lax.rem(flip(a, d), 2**l) * 8)
            push(ubuf.at[pl.ds(at, 8)], lurecv.at[pl.ds(8 * (SLOT[l] + d - 1), 8)], LU + l, flip(a, d), b)

    def spread(l, value):
        gath[l, pl.ds(own8, 8), :] = value
        mine = gath.at[l, pl.ds(own8, 8)]
        rowpeers(lambda row: push(mine, mine, AG + l, a, row))

    def load_sum(l):
        total = ubuf[pl.ds(at8(TOP[l] + lax.rem(a, 2**l) * 8), 8), :]
        if l:
            done(recv, LU + l, lurecv.at[pl.ds(0, 8 * (2**l - 1))])
            for d in range(1, 2**l):
                total = total + lurecv[8 * (SLOT[l] + d - 1) : 8 * (SLOT[l] + d), :]
        return total

    eye = lax.broadcasted_iota(jnp.int32, (8, 8), 0) == lax.broadcasted_iota(jnp.int32, (8, 8), 1)

    def pivots(l):
        return jnp.sum(jnp.where(eye, jnp.broadcast_to(wpiv[l : l + 1, :], (8, 8)), 0.0), axis=1, keepdims=True)

    def over_leaves(l, sem, rows, first_slot, slots, count):
        for d in range(1, count):
            at = at8(rows + lax.rem(flip(a, d), count) * 8)
            push(part.at[l, pl.ds(at, 8)], slots.at[pl.ds(8 * (first_slot + d - 1), 8)], sem, flip(a, d), b)

    def collect(sem, slots, first_slot, count, total):
        if count > 1:
            done(recv, sem, slots.at[pl.ds(0, 8 * (count - 1))])
            for d in range(1, count):
                total = total + slots[8 * (first_slot + d - 1) : 8 * (first_slot + d), :]
        return total

    def form_m(l):
        n = 2**l
        rows = 2 * n * 8
        done(recv, AY + l, aall.at[pl.ds(0, n), pl.ds(0, 24)])
        own = wcpl[LINK[l] : LINK[l] + rows, :]
        total = own
        for d in range(n):
            if d == 0:
                left = own
            else:
                if l == 2 or d == 1:
                    if not (l == 2 and d == 1):
                        first = 16 if d == 1 else 48
                        done(recv, BX + d, wcpl.at[pl.ds(first, 112 - first)])
                at = 96 * (d - 1) + LINK[l] - 16
                left = bpeer[at : at + rows, :]
            block = aall[n - 1 + lax.rem(flip(a, d), n)].reshape(256, 256)
            total = total + dot3(split(left), split(block))
        mbuf[LINK[l] : LINK[l] + rows, :] = total

    def keep_z(l, res, own_part):
        value = collect(YX + l, yrecv, SLOT[l], 2**l, res + own_part)
        value = value / pivots(l)
        at = at8(TOP[l] + lax.rem(a, 2**l) * 8)
        zbuf[pl.ds(at, 8), :] = value
        mine = zbuf.at[pl.ds(at, 8)]
        for d in range(1, 2**l):
            push(mine, mine, ZX + l, flip(a, d), b)
        return value

    below = None
    zs = []
    pending = None
    for l in range(LEVELS):
        n = 2**l
        res = wrhs[l] - load_sum(l)
        if l:
            res = res - below
        spread(l, res)
        if l in (1, 2):
            form_m(l)
        if pending is not None:
            zs.append(keep_z(l - 1, *pending))
        lhs = strict[TOP[l] : TOP[l] + 8 * n, :]
        if l < 3:
            lhs = jnp.concatenate([lhs, mbuf[LINK[l] : LINK[l] + 16 * n, :]], axis=0)
        lhs = split(lhs)
        done(recv, AG + l, gath.at[l, pl.ds(0, 248)])
        out = dot3(lhs, split(gath[l]))
        part[l, pl.ds(0, out.shape[0]), :] = out
        if l < 3:
            over_leaves(l, PX + l, 8 * n, SLOT[l + 1], precv, 2 * n)
        over_leaves(l, YX + l, 0, SLOT[l], yrecv, n)
        own_y = part[l, pl.ds(at8(lax.rem(a, n) * 8), 8), :]
        if l < 3:
            below = part[l, pl.ds(at8(8 * n + lax.rem(a, 2 * n) * 8), 8), :]
            below = collect(PX + l, precv, SLOT[l + 1], 2 * n, below)
        pending = (res, own_y)
    zs.append(keep_z(3, *pending))

    def fill(value, first):
        before = [jnp.zeros((first, 128), F32)] if first else []
        after = 128 - first - value.shape[0]
        return split(jnp.concatenate(before + [value] + ([jnp.zeros((after, 128), F32)] if after else []), axis=0))

    def own_half(l):
        n = 2**l
        if l:
            done(recv, ZX + l, zbuf.at[pl.ds(0, 8 * (n - 1))])
        return dot3(strict_t, fill(zbuf[TOP[l] : TOP[l] + 8 * n, :], TOP[l]))

    def reduce_rows(l, value, total):
        rsend[l] = value
        rrecv[l, pl.ds(own8, 8), :] = rsend[l, pl.ds(own8, 8), :]
        rowpeers(lambda row: push(rsend.at[l, pl.ds(at8(row * 8), 8)], rrecv.at[l, pl.ds(own8, 8)], RS + l, a, row))

    def reduced(l, total):
        done(recv, RS + l, rrecv.at[l, pl.ds(0, 248)])
        sums = [rrecv[l, 8 * s : 8 * s + 8, :] for s in range(NB)]
        while len(sums) > 1:
            sums = [sums[2 * k] + sums[2 * k + 1] for k in range(len(sums) // 2)]
        return total + sums[0]

    reduce_rows(3, own_half(3), None)
    m_t = jnp.concatenate([mbuf[0:112, :], jnp.zeros((16, 256), F32)], axis=0)
    m_t = split(jnp.concatenate([m_t[:, :128].T, m_t[:, 128:].T], axis=0))
    for l in reversed(range(LEVELS)):
        n = 2**l
        if l:
            ahead = own_half(l - 1)
        value = reduced(l, zs[l])
        out_win[l] = value
        at = at8(TOP[l] + lax.rem(a, n) * 8)
        xbuf[pl.ds(at, 8), :] = value
        mine = xbuf.at[pl.ds(at, 8)]
        for d in range(1, n):
            push(mine, mine, XX + l, flip(a, d), b)
        if l:
            done(recv, XX + l, xbuf.at[pl.ds(0, 8 * (n - 1))])
            level = xbuf[TOP[l] : TOP[l] + 8 * n, :]
            reduce_rows(l - 1, ahead - dot3(m_t, fill(level, LINK[l - 1])), None)
        block = xbuf.at[pl.ds(TOP[l], 8 * n)]
        there = xpath.at[pl.ds(at8(y * 128 + TOP[l]), 8 * n)]
        ypeers(lambda row: push(block, there, PY + l, a, row))
        xpath[pl.ds(at8(y * 128 + TOP[l]), 8 * n), :] = xbuf[TOP[l] : TOP[l] + 8 * n, :]

    for l in range(LEVELS):
        done(recv, PY + l, xpath.at[pl.ds(0, 24 * 2**l)])
    chosen = sel[0:32, 0:32].astype(BF16)
    pieces = []
    for j in range(16):
        ih, i8 = divmod(j, 8)
        pieces.append(jnp.concatenate([xpath[pl.ds(128 * (2 * h + ih) + i8, 16, stride=8), :] for h in range(2)], axis=0))
    pieces = split(jnp.concatenate(pieces, axis=1))
    picked = mm(chosen, pieces[0]) + mm(chosen, pieces[1])
    for j in range(16):
        psend[pl.ds(j, 32, stride=16), :] = picked[:, 128 * j : 128 * j + 128]
    precv2[pl.ds(own64, 64), :] = psend[pl.ds(own64, 64), :]
    zpeers(lambda z2, row: push(psend.at[pl.ds(at8(z2 * 64), 64)], precv2.at[pl.ds(own64, 64)], PICK, a, row))
    done(recv, PICK, precv2.at[pl.ds(0, 448)])
    rows = []
    for t in range(4):
        for i in range(16):
            ih, z2 = divmod(i, 8)
            at = z2 * 64 + t * 16 + ih * 8
            rows.append(precv2[at : at + 8, :])
    got = split(jnp.concatenate(rows, axis=0))
    for r in range(4):
        s = slice(128 * r, 128 * r + 128)
        yloc[s, :] = zloc[s, :] - dot3((ct_h[s, :], ct_l[s, :]), got)
    after = split(yloc[...])
    for r in range(4):
        s = slice(128 * r, 128 * r + 128)
        k = slice(128 * r, 512)
        out_loc[s, :] = yloc[s, :] + dot3((st_h[s, k], st_l[s, k]), (after[0][k], after[1][k]))

    done(send, PAT, patrecv.at[pl.ds(0, 7)])
    done(send, TERM, trecv.at[pl.ds(0, 448)])
    done(send, USUM, urecv.at[pl.ds(0, 384)])
    done(send, PICK, precv2.at[pl.ds(0, 448)])
    for l in range(LEVELS):
        n = 2**l
        if l < 3:
            done(send, AZ + l, aall.at[pl.ds(0, n), pl.ds(0, 7)])
            done(send, AY + l, aall.at[pl.ds(0, n), pl.ds(0, 24)])
            done(send, PX + l, precv.at[pl.ds(0, 8 * (2 * n - 1))])
        if l:
            done(send, LU + l, lurecv.at[pl.ds(0, 8 * (n - 1))])
            done(send, YX + l, yrecv.at[pl.ds(0, 8 * (n - 1))])
            done(send, ZX + l, zbuf.at[pl.ds(0, 8 * (n - 1))])
            done(send, XX + l, xbuf.at[pl.ds(0, 8 * (n - 1))])
        done(send, AG + l, gath.at[l, pl.ds(0, 248)])
        done(send, RS + l, rrecv.at[l, pl.ds(0, 248)])
        done(send, PY + l, xpath.at[pl.ds(0, 24 * n)])
    for d in range(1, 4):
        first = 16 if d == 1 else 48
        done(send, BX + d, wcpl.at[pl.ds(first, 112 - first)])


def shards(loc_rhs, loc_inverse, loc_coupling, loc_pivots, pattern, win_rhs, win_pivots, win_inverse, win_coupling):
    vmem = pl.BlockSpec(memory_space=pltpu.VMEM)
    specs = [vmem] * 9
    specs[4] = pl.BlockSpec(memory_space=pltpu.SMEM)
    out_loc, out_win = pl.pallas_call(
        kernel,
        out_shape=(jax.ShapeDtypeStruct((512, 128), F32), jax.ShapeDtypeStruct((LEVELS, 8, 128), F32)),
        in_specs=specs,
        out_specs=(vmem, vmem),
        scratch_shapes=[
            pltpu.VMEM((512, 512), BF16),
            pltpu.VMEM((512, 512), BF16),
            pltpu.VMEM((512, 512), BF16),
            pltpu.VMEM((512, 512), BF16),
            pltpu.VMEM((512, 128), F32),
            pltpu.VMEM((512, 128), F32),
            pltpu.VMEM((8, 4, 128), F32),
            pltpu.VMEM((128, 128), F32),
            pltpu.VMEM((512, 128), F32),
            pltpu.VMEM((512, 128), F32),
            pltpu.VMEM((512, 128), F32),
            pltpu.VMEM((512, 128), F32),
            pltpu.VMEM((128, 128), F32),
            pltpu.VMEM((88, 128), F32),
            pltpu.VMEM((128, 256), F32),
            pltpu.VMEM((7, NB, 8, 256), F32),
            pltpu.VMEM((288, 256), F32),
            pltpu.VMEM((112, 256), F32),
            pltpu.VMEM((LEVELS, 256, 128), F32),
            pltpu.VMEM((LEVELS, 96, 128), F32),
            pltpu.VMEM((88, 128), F32),
            pltpu.VMEM((88, 128), F32),
            pltpu.VMEM((120, 128), F32),
            pltpu.VMEM((120, 128), F32),
            pltpu.VMEM((LEVELS, 256, 128), F32),
            pltpu.VMEM((LEVELS, 256, 128), F32),
            pltpu.VMEM((512, 128), F32),
            pltpu.VMEM((512, 128), F32),
            pltpu.VMEM((512, 128), F32),
            pltpu.SemaphoreType.DMA((NSEM,)),
            pltpu.SemaphoreType.DMA((NSEM,)),
        ],
        compiler_params=pltpu.CompilerParams(collective_id=0, has_side_effects=True, vmem_limit_bytes=40 << 20),
    )(
        loc_rhs[0, 0], loc_inverse[0, 0], loc_coupling[0, 0], loc_pivots[0], pattern[0],
        win_rhs, win_pivots, win_inverse[0], win_coupling[0],
    )
    return out_loc[None, None], out_win


def solution(mesh):
    return jax.shard_map(
        shards,
        mesh=mesh,
        in_specs=(
            P("leaf", "row", None, None),
            P("leaf", "row", None, None),
            P("leaf", "row", None, None),
            P("leaf", "row", None),
            P("leaf", "row", None),
            P(None, ("leaf", "row"), None),
            P(None, ("leaf", "row")),
            P("row", None, "leaf"),
            P("row", None, "leaf"),
        ),
        out_specs=(P("leaf", "row", None, None), P(None, ("leaf", "row"), None)),
        check_vma=False,
    )
```

```python
import functools

import jax
import jax.numpy as jnp
from jax import lax
from jax.experimental import pallas as pl
from jax.experimental.pallas import tpu as pltpu
from jax.sharding import PartitionSpec as P

MESH = pl.DeviceIdType.MESH
F32 = jnp.float32
BF16 = jnp.bfloat16
NB, NY, NZ, NA, LEVELS = 32, 4, 8, 8, 4


def split(x):
    hi = x.astype(BF16)
    return hi, (x - hi.astype(F32)).astype(BF16)


def mm(left, right, dims=(((1,), (0,)), ((), ()))):
    return lax.dot_general(left, right, dims, preferred_element_type=F32)


def dot3(left, right):
    (lh, ll), (rh, rl) = left, right
    return mm(lh, rh) + (mm(lh, rl) + mm(ll, rh))


def flip(a, d):
    out = a
    for k in range(3):
        if (d >> k) & 1:
            out = out + (1 << k) * (1 - 2 * lax.rem(lax.div(a, 1 << k), 2))
    return out


def at8(value):
    return pl.multiple_of(value, 8)


TOP = [(2**l - 1) * 8 for l in range(LEVELS)]
LINK = [(2 * 2**l - 2) * 8 for l in range(LEVELS)]
SLOT = [0, 0, 1, 4]

PAT, TERM, USUM, PICK = 0, 1, 2, 3
AZ, AY, LU, AG, PX, YX, ZX, XX, RS, PY, BX = 4, 7, 10, 14, 18, 22, 26, 30, 34, 38, 42
U0, X0 = 46, 47
NSEM = 48


def kernel(rhs_in, inv_in, cpl_in, piv_in, pat_in, wrhs_in, wpiv_in, winv_in, wcpl_in, out_loc, out_win,
           rhs, inv, cpl, piv, pat, wrhs, wpiv, winv, wcpl, u0send, u0recv, x0all, loads,
           st_h, st_l, ct_h, ct_l, yloc, zloc, patrecv, sel, tsend, trecv, usend, urecv, ubuf, lurecv,
           strict, aall, bpeer, mbuf, gath, part, precv, yrecv, zbuf, xbuf,
           rsend, rrecv, xpath, psend, precv2, send, recv):
    a = lax.axis_index("leaf")
    b = lax.axis_index("row")
    y = lax.div(b, NZ)
    z = lax.rem(b, NZ)
    own8 = at8(b * 8)

    pairs = [(pat_in, pat), (rhs_in, rhs), (inv_in, inv), (winv_in, winv), (cpl_in, cpl),
             (wcpl_in, wcpl), (piv_in, piv), (wrhs_in, wrhs), (wpiv_in, wpiv)]
    fetch = [pltpu.make_async_copy(src, dst, loads.at[k]) for k, (src, dst) in enumerate(pairs)]
    for copy in fetch:
        copy.start()

    barrier = pltpu.get_barrier_semaphore()

    def greet(d, carry):
        pl.semaphore_signal(barrier, inc=1, device_id=(a, lax.rem(b + d, NB)), device_id_type=MESH)
        return carry

    lax.fori_loop(1, NB, greet, 0)
    for d in range(1, NA):
        pl.semaphore_signal(barrier, inc=1, device_id=(flip(a, d), b), device_id_type=MESH)

    def push(src, dst, sem, leaf, row):
        pltpu.make_async_remote_copy(
            src_ref=src, dst_ref=dst, send_sem=send.at[sem], recv_sem=recv.at[sem],
            device_id=(leaf, row), device_id_type=MESH,
        ).start()

    def done(which, sem, view):
        pltpu.make_async_copy(view, view, which.at[sem]).wait()

    def zpeers(body):
        def step(d, carry):
            z2 = lax.rem(z + d, NZ)
            body(z2, y * NZ + z2)
            return carry

        lax.fori_loop(1, NZ, step, 0)

    def ypeers(body):
        def step(d, carry):
            body(lax.rem(b + d * NZ, NB))
            return carry

        lax.fori_loop(1, NY, step, 0)

    def rowpeers(body):
        def step(d, carry):
            body(lax.rem(b + d, NB))
            return carry

        lax.fori_loop(1, NB, step, 0)

    sel[...] = jnp.zeros((128, 128), F32)
    xpath[...] = jnp.zeros((512, 128), F32)

    fetch[3].wait()
    for l in range(LEVELS):
        n = 2**l * 8
        rows = lax.broadcasted_iota(jnp.int32, (n, 256), 0)
        cols = lax.broadcasted_iota(jnp.int32, (n, 256), 1)
        row_id = lax.div(rows, 8) * 256 + b * 8 + lax.rem(rows, 8)
        col_id = lax.rem(a, 2**l) * 256 + cols
        block = jnp.where(col_id < row_id, winv[TOP[l] : TOP[l] + n, :], 0.0)
        strict[TOP[l] : TOP[l] + n, :] = block
        if l < 3:
            for q in range(2**l):
                aall[2**l - 1 + q, b] = block[8 * q : 8 * q + 8]
    strict[120:128, :] = jnp.zeros((8, 256), F32)

    fetch[0].wait()
    lane = lax.broadcasted_iota(jnp.int32, (1, 128), 1)
    base = []
    for t in range(4):
        tile = pat[0, t]
        base.append([jnp.where(jnp.full((1, 128), tile, jnp.int32) == p, 1.0, 0.0).astype(F32) for p in range(2)])
        mark = lax.rem(tile, 2) * 16 + lax.div(tile, 2)
        patrecv[z, t : t + 1, :] = jnp.where(lane == mark, 1.0, 0.0).astype(F32)

    low_row = lax.broadcasted_iota(jnp.int32, (128, 128), 0)
    low_col = lax.broadcasted_iota(jnp.int32, (128, 128), 1)
    low = low_col < low_row
    fetch[1].wait()
    fetch[2].wait()
    right = split(rhs[...])
    for r in range(4):
        acc = rhs[128 * r : 128 * r + 128, :]
        diag = jnp.where(low, inv[128 * r : 128 * r + 128, 128 * r : 128 * r + 128], 0.0)
        acc = acc + dot3(split(diag), (right[0][128 * r : 128 * r + 128], right[1][128 * r : 128 * r + 128]))
        if r:
            acc = acc + dot3(split(inv[128 * r : 128 * r + 128, : 128 * r]), (right[0][: 128 * r], right[1][: 128 * r]))
        yloc[128 * r : 128 * r + 128, :] = acc

    pl.semaphore_wait(barrier, NB - 1 + NA - 1)

    zpeers(lambda z2, row: push(patrecv.at[z], patrecv.at[z], PAT, a, row))
    zpeers(lambda z2, row: push(aall.at[pl.ds(0, 1), b], aall.at[pl.ds(0, 1), b], AZ, a, row))

    solved = split(yloc[...])
    fetch[4].wait()
    low0, low1 = 0.0, 0.0
    for t in range(4):
        term = dot3(split(cpl[128 * t : 128 * t + 128, :]), solved)
        low0 = low0 + base[t][0] * term
        low1 = low1 + base[t][1] * term
        for i in range(16):
            ih, z2 = divmod(i, 8)
            at = z2 * 64 + t * 16 + ih * 8
            tsend[at : at + 8, :] = term[8 * i : 8 * i + 8]
    u0send[0:128, :] = low0
    u0send[128:256, :] = low1
    rowpeers(lambda row: push(u0send.at[pl.ds(at8(row * 8), 8)], u0recv.at[pl.ds(own8, 8)], U0, a, row))
    u0recv[pl.ds(own8, 8), :] = u0send[pl.ds(own8, 8), :]
    own64 = at8(z * 64)
    zpeers(lambda z2, row: push(tsend.at[pl.ds(at8(z2 * 64), 64)], trecv.at[pl.ds(own64, 64)], TERM, a, row))
    trecv[pl.ds(own64, 64), :] = tsend[pl.ds(own64, 64), :]
    fetch[5].wait()

    for l in (1, 2):
        n = 2**l
        zpeers(lambda z2, row: push(aall.at[pl.ds(n - 1, n), b], aall.at[pl.ds(n - 1, n), b], AZ + l, a, row))
    for d in range(1, 4):
        first = 16 if d == 1 else 48
        push(wcpl.at[pl.ds(first, 112 - first)], bpeer.at[pl.ds(96 * (d - 1) + first - 16, 112 - first)], BX + d, flip(a, d), b)

    def forward_a(l):
        n = 2**l
        done(recv, AZ + l, aall.at[pl.ds(0, n), pl.ds(0, 7)])
        slab = aall.at[pl.ds(n - 1, n), pl.ds(y * NZ, NZ)]
        ypeers(lambda row: push(slab, slab, AY + l, a, row))

    forward_a(0)

    for r in range(4):
        for c in range(4):
            blk = cpl[128 * r : 128 * r + 128, 128 * c : 128 * c + 128].T
            h, lo = split(blk)
            ct_h[128 * c : 128 * c + 128, 128 * r : 128 * r + 128] = h
            ct_l[128 * c : 128 * c + 128, 128 * r : 128 * r + 128] = lo
            if c <= r:
                blk = inv[128 * r : 128 * r + 128, 128 * c : 128 * c + 128]
                if c == r:
                    blk = jnp.where(low, blk, 0.0)
                h, lo = split(blk.T)
                st_h[128 * c : 128 * c + 128, 128 * r : 128 * r + 128] = h
                st_l[128 * c : 128 * c + 128, 128 * r : 128 * r + 128] = lo
    strict_t = jnp.concatenate([strict[:, :128].T, strict[:, 128:].T], axis=0)
    strict_t = split(strict_t)
    fetch[6].wait()
    wide = jnp.broadcast_to(piv[...], (128, 512))
    for r in range(4):
        zloc[128 * r : 128 * r + 128, :] = yloc[128 * r : 128 * r + 128, :] / wide[:, 128 * r : 128 * r + 128].T

    def tree(ref):
        sums = [ref[8 * s : 8 * s + 8, :] for s in range(NB)]
        while len(sums) > 1:
            sums = [sums[2 * k] + sums[2 * k + 1] for k in range(len(sums) // 2)]
        return sums[0]

    def place_terms():
        done(recv, PAT, patrecv.at[pl.ds(0, 7)])
        for s in range(8):
            sel[4 * s : 4 * s + 4, :] = patrecv[s]
        chosen_t = sel[...].T[:32, :32].astype(BF16)
        done(recv, TERM, trecv.at[pl.ds(0, 448)])
        cols = split(jnp.concatenate([trecv[pl.ds(j, 32, stride=16), :] for j in range(16)], axis=1))
        placed = mm(chosen_t, cols[0]) + mm(chosen_t, cols[1])
        for j in range(16):
            ih, i8 = divmod(j, 8)
            for h in range(2):
                usend[pl.ds(128 * (2 * h + ih) + i8, 16, stride=8), :] = placed[16 * h : 16 * h + 16, 128 * j : 128 * j + 128]
        own128 = at8(y * 128)
        ypeers(lambda row: push(usend.at[pl.ds(at8(lax.div(row, NZ) * 128 + 8), 112)], urecv.at[pl.ds(at8(own128 + 8), 112)], USUM, a, row))
        urecv[pl.ds(own128, 128), :] = usend[pl.ds(own128, 128), :]

    def sum_terms():
        done(recv, USUM, urecv.at[pl.ds(0, 336)])
        ubuf[8:120, :] = (urecv[8:120, :] + urecv[136:248, :]) + (urecv[264:376, :] + urecv[392:504, :])
        for l in range(1, LEVELS):
            for d in range(1, 2**l):
                at = at8(TOP[l] + lax.rem(flip(a, d), 2**l) * 8)
                push(ubuf.at[pl.ds(at, 8)], lurecv.at[pl.ds(8 * (SLOT[l] + d - 1), 8)], LU + l, flip(a, d), b)

    def form_m0():
        done(recv, AY, aall.at[pl.ds(0, 1), pl.ds(0, 24)])
        mbuf[0:16, :] = wcpl[0:16, :] + dot3(split(wcpl[0:16, :]), split(aall[0].reshape(256, 256)))

    def spread(l, value):
        gath[l, pl.ds(own8, 8), :] = value
        mine = gath.at[l, pl.ds(own8, 8)]
        rowpeers(lambda row: push(mine, mine, AG + l, a, row))

    def load_sum(l):
        total = ubuf[pl.ds(at8(TOP[l] + lax.rem(a, 2**l) * 8), 8), :]
        done(recv, LU + l, lurecv.at[pl.ds(0, 8 * (2**l - 1))])
        for d in range(1, 2**l):
            total = total + lurecv[8 * (SLOT[l] + d - 1) : 8 * (SLOT[l] + d), :]
        return total

    eye = lax.broadcasted_iota(jnp.int32, (8, 8), 0) == lax.broadcasted_iota(jnp.int32, (8, 8), 1)

    def pivots(l):
        return jnp.sum(jnp.where(eye, jnp.broadcast_to(wpiv[l : l + 1, :], (8, 8)), 0.0), axis=1, keepdims=True)

    def over_leaves(l, sem, rows, first_slot, slots, count):
        for d in range(1, count):
            at = at8(rows + lax.rem(flip(a, d), count) * 8)
            push(part.at[l, pl.ds(at, 8)], slots.at[pl.ds(8 * (first_slot + d - 1), 8)], sem, flip(a, d), b)

    def collect(sem, slots, first_slot, count, total):
        if count > 1:
            done(recv, sem, slots.at[pl.ds(0, 8 * (count - 1))])
            for d in range(1, count):
                total = total + slots[8 * (first_slot + d - 1) : 8 * (first_slot + d), :]
        return total

    def form_m(l):
        n = 2**l
        rows = 2 * n * 8
        done(recv, AY + l, aall.at[pl.ds(0, n), pl.ds(0, 24)])
        own = wcpl[LINK[l] : LINK[l] + rows, :]
        total = own
        for d in range(n):
            if d == 0:
                left = own
            else:
                if l == 2 or d == 1:
                    if not (l == 2 and d == 1):
                        first = 16 if d == 1 else 48
                        done(recv, BX + d, wcpl.at[pl.ds(first, 112 - first)])
                at = 96 * (d - 1) + LINK[l] - 16
                left = bpeer[at : at + rows, :]
            block = aall[n - 1 + lax.rem(flip(a, d), n)].reshape(256, 256)
            total = total + dot3(split(left), split(block))
        mbuf[LINK[l] : LINK[l] + rows, :] = total

    def keep_z(l, res, own_part):
        value = collect(YX + l, yrecv, SLOT[l], 2**l, res + own_part)
        value = value / pivots(l)
        at = at8(TOP[l] + lax.rem(a, 2**l) * 8)
        zbuf[pl.ds(at, 8), :] = value
        mine = zbuf.at[pl.ds(at, 8)]
        for d in range(1, 2**l):
            push(mine, mine, ZX + l, flip(a, d), b)
        return value

    below = None
    zs = []
    pending = None
    fetch[7].wait()
    fetch[8].wait()
    for l in range(LEVELS):
        n = 2**l
        if l:
            res = wrhs[l] - load_sum(l) - below
        else:
            done(recv, U0, u0recv.at[pl.ds(0, 248)])
            res = wrhs[0] - tree(u0recv)
        spread(l, res)
        if l == 0:
            place_terms()
            forward_a(1)
            form_m0()
            forward_a(2)
        if l in (1, 2):
            form_m(l)
        if pending is not None:
            zs.append(keep_z(l - 1, *pending))
        lhs = strict[TOP[l] : TOP[l] + 8 * n, :]
        if l < 3:
            lhs = jnp.concatenate([lhs, mbuf[LINK[l] : LINK[l] + 16 * n, :]], axis=0)
        lhs = split(lhs)
        done(recv, AG + l, gath.at[l, pl.ds(0, 248)])
        out = dot3(lhs, split(gath[l]))
        part[l, pl.ds(0, out.shape[0]), :] = out
        if l < 3:
            over_leaves(l, PX + l, 8 * n, SLOT[l + 1], precv, 2 * n)
        over_leaves(l, YX + l, 0, SLOT[l], yrecv, n)
        own_y = part[l, pl.ds(at8(lax.rem(a, n) * 8), 8), :]
        if l == 0:
            sum_terms()
        if l < 3:
            below = part[l, pl.ds(at8(8 * n + lax.rem(a, 2 * n) * 8), 8), :]
            below = collect(PX + l, precv, SLOT[l + 1], 2 * n, below)
        pending = (res, own_y)
    zs.append(keep_z(3, *pending))

    def fill(value, first):
        before = [jnp.zeros((first, 128), F32)] if first else []
        after = 128 - first - value.shape[0]
        return split(jnp.concatenate(before + [value] + ([jnp.zeros((after, 128), F32)] if after else []), axis=0))

    def own_half(l):
        n = 2**l
        if l:
            done(recv, ZX + l, zbuf.at[pl.ds(0, 8 * (n - 1))])
        return dot3(strict_t, fill(zbuf[TOP[l] : TOP[l] + 8 * n, :], TOP[l]))

    def reduce_rows(l, value, total):
        rsend[l] = value
        rrecv[l, pl.ds(own8, 8), :] = rsend[l, pl.ds(own8, 8), :]
        rowpeers(lambda row: push(rsend.at[l, pl.ds(at8(row * 8), 8)], rrecv.at[l, pl.ds(own8, 8)], RS + l, a, row))

    def reduced(l, total):
        done(recv, RS + l, rrecv.at[l, pl.ds(0, 248)])
        return total + tree(rrecv.at[l])

    reduce_rows(3, own_half(3), None)
    m_t = jnp.concatenate([mbuf[0:112, :], jnp.zeros((16, 256), F32)], axis=0)
    m_t = split(jnp.concatenate([m_t[:, :128].T, m_t[:, 128:].T], axis=0))
    for l in reversed(range(LEVELS)):
        n = 2**l
        if l:
            ahead = own_half(l - 1)
        else:
            for m in range(1, LEVELS):
                done(recv, PY + m, xpath.at[pl.ds(0, 24 * 2**m)])
            chosen = sel[0:32, 0:32].astype(BF16)
            pieces = []
            for j in range(16):
                ih, i8 = divmod(j, 8)
                pieces.append(jnp.concatenate([xpath[pl.ds(128 * (2 * h + ih) + i8, 16, stride=8), :] for h in range(2)], axis=0))
            pieces = split(jnp.concatenate(pieces, axis=1))
            picked = mm(chosen, pieces[0]) + mm(chosen, pieces[1])
            for j in range(16):
                psend[pl.ds(j, 32, stride=16), :] = picked[:, 128 * j : 128 * j + 128]
            zpeers(lambda z2, row: push(psend.at[pl.ds(at8(z2 * 64), 64)], precv2.at[pl.ds(own64, 64)], PICK, a, row))
            precv2[pl.ds(own64, 64), :] = psend[pl.ds(own64, 64), :]
        value = reduced(l, zs[l])
        if l:
            at = at8(TOP[l] + lax.rem(a, n) * 8)
            xbuf[pl.ds(at, 8), :] = value
            mine = xbuf.at[pl.ds(at, 8)]
            for d in range(1, n):
                push(mine, mine, XX + l, flip(a, d), b)
            out_win[l] = value
            done(recv, XX + l, xbuf.at[pl.ds(0, 8 * (n - 1))])
            level = xbuf[TOP[l] : TOP[l] + 8 * n, :]
            reduce_rows(l - 1, ahead - dot3(m_t, fill(level, LINK[l - 1])), None)
            block = xbuf.at[pl.ds(TOP[l], 8 * n)]
            there = xpath.at[pl.ds(at8(y * 128 + TOP[l]), 8 * n)]
            ypeers(lambda row: push(block, there, PY + l, a, row))
            xpath[pl.ds(at8(y * 128 + TOP[l]), 8 * n), :] = level
        else:
            x0all[pl.ds(own8, 8), :] = value
            mine = x0all.at[pl.ds(own8, 8)]
            rowpeers(lambda row: push(mine, mine, X0, a, row))
            out_win[0] = value

    done(recv, PICK, precv2.at[pl.ds(0, 448)])
    done(recv, X0, x0all.at[pl.ds(0, 248)])
    rows = []
    for t in range(4):
        for i in range(16):
            ih, z2 = divmod(i, 8)
            at = z2 * 64 + t * 16 + ih * 8
            here = base[t][0] * x0all[8 * i : 8 * i + 8, :] + base[t][1] * x0all[128 + 8 * i : 136 + 8 * i, :]
            rows.append(precv2[at : at + 8, :] + here)
    got = split(jnp.concatenate(rows, axis=0))
    for r in range(4):
        s = slice(128 * r, 128 * r + 128)
        yloc[s, :] = zloc[s, :] - dot3((ct_h[s, :], ct_l[s, :]), got)
    after = split(yloc[...])
    for r in range(4):
        s = slice(128 * r, 128 * r + 128)
        k = slice(128 * r, 512)
        out_loc[s, :] = yloc[s, :] + dot3((st_h[s, k], st_l[s, k]), (after[0][k], after[1][k]))

    done(send, PAT, patrecv.at[pl.ds(0, 7)])
    done(send, TERM, trecv.at[pl.ds(0, 448)])
    done(send, USUM, urecv.at[pl.ds(0, 336)])
    done(send, U0, u0recv.at[pl.ds(0, 248)])
    done(send, X0, x0all.at[pl.ds(0, 248)])
    done(send, PICK, precv2.at[pl.ds(0, 448)])
    for l in range(LEVELS):
        n = 2**l
        if l < 3:
            done(send, AZ + l, aall.at[pl.ds(0, n), pl.ds(0, 7)])
            done(send, AY + l, aall.at[pl.ds(0, n), pl.ds(0, 24)])
            done(send, PX + l, precv.at[pl.ds(0, 8 * (2 * n - 1))])
        if l:
            done(send, LU + l, lurecv.at[pl.ds(0, 8 * (n - 1))])
            done(send, YX + l, yrecv.at[pl.ds(0, 8 * (n - 1))])
            done(send, ZX + l, zbuf.at[pl.ds(0, 8 * (n - 1))])
            done(send, XX + l, xbuf.at[pl.ds(0, 8 * (n - 1))])
        done(send, AG + l, gath.at[l, pl.ds(0, 248)])
        done(send, RS + l, rrecv.at[l, pl.ds(0, 248)])
        if l:
            done(send, PY + l, xpath.at[pl.ds(0, 24 * n)])
    for d in range(1, 4):
        first = 16 if d == 1 else 48
        done(send, BX + d, wcpl.at[pl.ds(first, 112 - first)])


def shards(loc_rhs, loc_inverse, loc_coupling, loc_pivots, pattern, win_rhs, win_pivots, win_inverse, win_coupling):
    vmem = pl.BlockSpec(memory_space=pltpu.VMEM)
    specs = [pl.BlockSpec(memory_space=pl.ANY)] * 9
    out_loc, out_win = pl.pallas_call(
        kernel,
        out_shape=(jax.ShapeDtypeStruct((512, 128), F32), jax.ShapeDtypeStruct((LEVELS, 8, 128), F32)),
        in_specs=specs,
        out_specs=(vmem, vmem),
        scratch_shapes=[
            pltpu.VMEM((512, 128), F32),
            pltpu.VMEM((512, 512), F32),
            pltpu.VMEM((512, 512), F32),
            pltpu.VMEM((1, 512), F32),
            pltpu.SMEM((1, 4), jnp.int32),
            pltpu.VMEM((LEVELS, 8, 128), F32),
            pltpu.VMEM((LEVELS, 8), F32),
            pltpu.VMEM((120, 256), F32),
            pltpu.VMEM((112, 256), F32),
            pltpu.VMEM((256, 128), F32),
            pltpu.VMEM((256, 128), F32),
            pltpu.VMEM((256, 128), F32),
            pltpu.SemaphoreType.DMA((9,)),
            pltpu.VMEM((512, 512), BF16),
            pltpu.VMEM((512, 512), BF16),
            pltpu.VMEM((512, 512), BF16),
            pltpu.VMEM((512, 512), BF16),
            pltpu.VMEM((512, 128), F32),
            pltpu.VMEM((512, 128), F32),
            pltpu.VMEM((8, 4, 128), F32),
            pltpu.VMEM((128, 128), F32),
            pltpu.VMEM((512, 128), F32),
            pltpu.VMEM((512, 128), F32),
            pltpu.VMEM((512, 128), F32),
            pltpu.VMEM((512, 128), F32),
            pltpu.VMEM((128, 128), F32),
            pltpu.VMEM((88, 128), F32),
            pltpu.VMEM((128, 256), F32),
            pltpu.VMEM((7, NB, 8, 256), F32),
            pltpu.VMEM((288, 256), F32),
            pltpu.VMEM((112, 256), F32),
            pltpu.VMEM((LEVELS, 256, 128), F32),
            pltpu.VMEM((LEVELS, 96, 128), F32),
            pltpu.VMEM((88, 128), F32),
            pltpu.VMEM((88, 128), F32),
            pltpu.VMEM((120, 128), F32),
            pltpu.VMEM((120, 128), F32),
            pltpu.VMEM((LEVELS, 256, 128), F32),
            pltpu.VMEM((LEVELS, 256, 128), F32),
            pltpu.VMEM((512, 128), F32),
            pltpu.VMEM((512, 128), F32),
            pltpu.VMEM((512, 128), F32),
            pltpu.SemaphoreType.DMA((NSEM,)),
            pltpu.SemaphoreType.DMA((NSEM,)),
        ],
        compiler_params=pltpu.CompilerParams(collective_id=0, has_side_effects=True),
    )(
        loc_rhs[0, 0], loc_inverse[0, 0], loc_coupling[0, 0], loc_pivots[0], pattern[0],
        win_rhs, win_pivots, win_inverse[0], win_coupling[0],
    )
    return out_loc[None, None], out_win


def solution(mesh):
    return jax.shard_map(
        shards,
        mesh=mesh,
        in_specs=(
            P("leaf", "row", None, None),
            P("leaf", "row", None, None),
            P("leaf", "row", None, None),
            P("leaf", "row", None),
            P("leaf", "row", None),
            P(None, ("leaf", "row"), None),
            P(None, ("leaf", "row")),
            P("row", None, "leaf"),
            P("row", None, "leaf"),
        ),
        out_specs=(P("leaf", "row", None, None), P(None, ("leaf", "row"), None)),
        check_vma=False,
    )
```

```python
import functools

import jax
import jax.numpy as jnp
from jax import lax
from jax.experimental import pallas as pl
from jax.experimental.pallas import tpu as pltpu
from jax.sharding import PartitionSpec as P

MESH = pl.DeviceIdType.MESH
F32 = jnp.float32
BF16 = jnp.bfloat16
NB, NY, NZ, NA, LEVELS = 32, 4, 8, 8, 4


def split(x):
    hi = x.astype(BF16)
    return hi, (x - hi.astype(F32)).astype(BF16)


def mm(left, right, dims=(((1,), (0,)), ((), ()))):
    return lax.dot_general(left, right, dims, preferred_element_type=F32)


def dot3(left, right):
    (lh, ll), (rh, rl) = left, right
    n = rh.shape[1]
    if n != 128:
        return mm(lh, rh) + (mm(lh, rl) + mm(ll, rh))
    both = mm(lh, jnp.concatenate([rh, rl], axis=1))
    return both[:, :n] + (both[:, n:] + mm(ll, rh))


def flip(a, d):
    out = a
    for k in range(3):
        if (d >> k) & 1:
            out = out + (1 << k) * (1 - 2 * lax.rem(lax.div(a, 1 << k), 2))
    return out


def at8(value):
    return pl.multiple_of(value, 8)


TOP = [(2**l - 1) * 8 for l in range(LEVELS)]
LINK = [(2 * 2**l - 2) * 8 for l in range(LEVELS)]
SLOT = [0, 0, 1, 4]

PAT, TERM, USUM, PICK = 0, 1, 2, 3
AZ, AY, LU, AG, PX, YX, ZX, XX, RS, PY, BX = 4, 7, 10, 14, 18, 22, 26, 30, 34, 38, 42
U0, X1, MZ, MY, ZA = 46, 47, 48, 49, 50
NSEM = 51


def kernel(rhs_in, inv_in, cpl_in, piv_in, pat_in, wrhs_in, wpiv_in, winv_in, wcpl_in, out_loc, out_win,
           rhs, inv, cpl, piv, pat, wrhs, wpiv, winv, wcpl, u0send, u0recv, x0all, x1all, z0all, c0, m0all, m0t_h, m0t_l, loads,
           st_h, st_l, ct_h, ct_l, yloc, zloc, patrecv, sel, tsend, trecv, usend, urecv, ubuf, lurecv,
           strict, aall, bpeer, mbuf, gath, part, precv, yrecv, zbuf, xbuf,
           rsend, rrecv, xpath, psend, precv2, send, recv):
    a = lax.axis_index("leaf")
    b = lax.axis_index("row")
    y = lax.div(b, NZ)
    z = lax.rem(b, NZ)
    own8 = at8(b * 8)

    pairs = [(pat_in, pat), (rhs_in, rhs), (inv_in, inv), (winv_in, winv), (cpl_in, cpl),
             (wcpl_in, wcpl), (piv_in, piv), (wrhs_in, wrhs), (wpiv_in, wpiv)]
    fetch = [pltpu.make_async_copy(src, dst, loads.at[k]) for k, (src, dst) in enumerate(pairs)]
    for copy in fetch:
        copy.start()

    barrier = pltpu.get_barrier_semaphore()

    def greet(d, carry):
        pl.semaphore_signal(barrier, inc=1, device_id=(a, lax.rem(b + d, NB)), device_id_type=MESH)
        return carry

    lax.fori_loop(1, NB, greet, 0)
    for d in range(1, NA):
        pl.semaphore_signal(barrier, inc=1, device_id=(flip(a, d), b), device_id_type=MESH)

    def push(src, dst, sem, leaf, row):
        pltpu.make_async_remote_copy(
            src_ref=src, dst_ref=dst, send_sem=send.at[sem], recv_sem=recv.at[sem],
            device_id=(leaf, row), device_id_type=MESH,
        ).start()

    views = {PAT: patrecv.at[pl.ds(0, 7)], TERM: trecv.at[pl.ds(0, 448)], USUM: urecv.at[pl.ds(0, 336)],
             PICK: precv2.at[pl.ds(0, 448)], U0: u0recv.at[pl.ds(0, 248)],
             X1: x1all.at[:, pl.ds(0, 31)], MZ: m0all.at[:, pl.ds(0, 7)], MY: m0all.at[:, pl.ds(0, 24)],
             ZA: z0all.at[pl.ds(0, 248)]}
    for l in range(LEVELS):
        n = 2**l
        views[AG + l] = gath.at[l, pl.ds(0, 248)]
        if l < 3:
            views[AZ + l] = aall.at[pl.ds(0, n), pl.ds(0, 7)]
            views[AY + l] = aall.at[pl.ds(0, n), pl.ds(0, 24)]
            views[PX + l] = precv.at[pl.ds(0, 8 * (2 * n - 1))]
        if l:
            views[RS + l] = rrecv.at[l, pl.ds(0, 248)]
            views[LU + l] = lurecv.at[pl.ds(0, 8 * (n - 1))]
            views[YX + l] = yrecv.at[pl.ds(0, 8 * (n - 1))]
            views[ZX + l] = zbuf.at[pl.ds(0, 8 * (n - 1))]
            views[XX + l] = xbuf.at[pl.ds(0, 8 * (n - 1))]
        if l > 1:
            views[PY + l] = xpath.at[pl.ds(0, 24 * n)]
    for d in range(1, 4):
        first = 16 if d == 1 else 48
        views[BX + d] = wcpl.at[pl.ds(first, 112 - first)]

    def done(which, sem):
        pltpu.make_async_copy(views[sem], views[sem], which.at[sem]).wait()

    def around(k, n):
        return n // 2 + lax.div(k + 1, 2) * (1 - 2 * lax.rem(k, 2))

    def zpeers(body):
        def step(k, carry):
            z2 = lax.rem(z + around(k, NZ), NZ)
            body(z2, y * NZ + z2)
            return carry

        lax.fori_loop(0, NZ - 1, step, 0)

    def ypeers(body):
        def step(k, carry):
            body(lax.rem(y + around(k, NY), NY) * NZ + z)
            return carry

        lax.fori_loop(0, NY - 1, step, 0)

    def rowpeers(body):
        def step(k, carry):
            y2 = lax.rem(y + around(lax.rem(k, NY), NY), NY)
            z2 = lax.rem(z + around(lax.div(k, NY), NZ), NZ)
            body(y2 * NZ + z2)
            return carry

        lax.fori_loop(0, NB - 1, step, 0)

    sel[...] = jnp.zeros((128, 128), F32)
    xpath[...] = jnp.zeros((512, 128), F32)

    fetch[3].wait()
    for l in range(LEVELS):
        n = 2**l * 8
        rows = lax.broadcasted_iota(jnp.int32, (n, 256), 0)
        cols = lax.broadcasted_iota(jnp.int32, (n, 256), 1)
        row_id = lax.div(rows, 8) * 256 + b * 8 + lax.rem(rows, 8)
        col_id = lax.rem(a, 2**l) * 256 + cols
        block = jnp.where(col_id < row_id, winv[TOP[l] : TOP[l] + n, :], 0.0)
        strict[TOP[l] : TOP[l] + n, :] = block
        if l < 3:
            for q in range(2**l):
                aall[2**l - 1 + q, b] = block[8 * q : 8 * q + 8]
    strict[120:128, :] = jnp.zeros((8, 256), F32)

    fetch[0].wait()
    lane = lax.broadcasted_iota(jnp.int32, (1, 128), 1)
    base = []
    for t in range(4):
        tile = pat[0, t]
        base.append([jnp.where(jnp.full((1, 128), tile, jnp.int32) == p, 1.0, 0.0).astype(F32) for p in range(6)])
        mark = lax.rem(tile, 2) * 16 + lax.div(tile, 2)
        patrecv[z, t : t + 1, :] = jnp.where(lane == mark, 1.0, 0.0).astype(F32)

    low_row = lax.broadcasted_iota(jnp.int32, (128, 128), 0)
    low_col = lax.broadcasted_iota(jnp.int32, (128, 128), 1)
    low = low_col < low_row
    fetch[1].wait()
    fetch[2].wait()
    right = split(rhs[...])
    for r in range(4):
        acc = rhs[128 * r : 128 * r + 128, :]
        diag = jnp.where(low, inv[128 * r : 128 * r + 128, 128 * r : 128 * r + 128], 0.0)
        acc = acc + dot3(split(diag), (right[0][128 * r : 128 * r + 128], right[1][128 * r : 128 * r + 128]))
        if r:
            acc = acc + dot3(split(inv[128 * r : 128 * r + 128, : 128 * r]), (right[0][: 128 * r], right[1][: 128 * r]))
        yloc[128 * r : 128 * r + 128, :] = acc

    pl.semaphore_wait(barrier, NB - 1 + NA - 1)

    zpeers(lambda z2, row: push(patrecv.at[z], patrecv.at[z], PAT, a, row))
    for l in range(3):
        n = 2**l
        zpeers(lambda z2, row: push(aall.at[pl.ds(n - 1, n), b], aall.at[pl.ds(n - 1, n), b], AZ + l, a, row))

    solved = split(yloc[...])
    fetch[4].wait()
    low0, low1 = 0.0, 0.0
    for t in range(4):
        term = dot3(split(cpl[128 * t : 128 * t + 128, :]), solved)
        low0 = low0 + base[t][0] * term
        low1 = low1 + base[t][1] * term
        for i in range(16):
            ih, z2 = divmod(i, 8)
            at = z2 * 64 + t * 16 + ih * 8
            tsend[at : at + 8, :] = term[8 * i : 8 * i + 8]
    u0send[0:128, :] = low0
    u0send[128:256, :] = low1
    rowpeers(lambda row: push(u0send.at[pl.ds(at8(row * 8), 8)], u0recv.at[pl.ds(own8, 8)], U0, a, row))
    u0recv[pl.ds(own8, 8), :] = u0send[pl.ds(own8, 8), :]
    own64 = at8(z * 64)
    zpeers(lambda z2, row: push(tsend.at[pl.ds(at8(z2 * 64), 64)], trecv.at[pl.ds(own64, 64)], TERM, a, row))
    trecv[pl.ds(own64, 64), :] = tsend[pl.ds(own64, 64), :]
    fetch[5].wait()

    for d in range(1, 4):
        first = 16 if d == 1 else 48
        push(wcpl.at[pl.ds(first, 112 - first)], bpeer.at[pl.ds(96 * (d - 1) + first - 16, 112 - first)], BX + d, flip(a, d), b)

    def forward_a(l, first, count):
        slab = aall.at[pl.ds(2**l - 1 + first, count), pl.ds(y * NZ, NZ)]
        ypeers(lambda row: push(slab, slab, AY + l, a, row))

    done(recv, AZ)
    forward_a(0, 0, 1)
    done(recv, AZ + 1)
    forward_a(1, 0, 2)

    for r in range(4):
        for c in range(4):
            blk = cpl[128 * r : 128 * r + 128, 128 * c : 128 * c + 128].T
            h, lo = split(blk)
            ct_h[128 * c : 128 * c + 128, 128 * r : 128 * r + 128] = h
            ct_l[128 * c : 128 * c + 128, 128 * r : 128 * r + 128] = lo
            if c <= r:
                blk = inv[128 * r : 128 * r + 128, 128 * c : 128 * c + 128]
                if c == r:
                    blk = jnp.where(low, blk, 0.0)
                h, lo = split(blk.T)
                st_h[128 * c : 128 * c + 128, 128 * r : 128 * r + 128] = h
                st_l[128 * c : 128 * c + 128, 128 * r : 128 * r + 128] = lo
    strict_t = jnp.concatenate([strict[:, :128].T, strict[:, 128:].T], axis=0)
    strict_t = split(strict_t)
    fetch[6].wait()
    wide = jnp.broadcast_to(piv[...], (128, 512))
    for r in range(4):
        zloc[128 * r : 128 * r + 128, :] = yloc[128 * r : 128 * r + 128, :] / wide[:, 128 * r : 128 * r + 128].T

    def tree(ref):
        sums = [ref[8 * s : 8 * s + 8, :] for s in range(NB)]
        while len(sums) > 1:
            sums = [sums[2 * k] + sums[2 * k + 1] for k in range(len(sums) // 2)]
        return sums[0]

    def place_terms():
        done(recv, PAT)
        for s in range(8):
            sel[4 * s : 4 * s + 4, :] = patrecv[s]
        chosen_t = sel[...].T[:32, :32].astype(BF16)
        done(recv, TERM)
        cols = split(jnp.concatenate([trecv[pl.ds(j, 32, stride=16), :] for j in range(16)], axis=1))
        placed = mm(chosen_t, cols[0]) + mm(chosen_t, cols[1])
        for j in range(16):
            ih, i8 = divmod(j, 8)
            for h in range(2):
                usend[pl.ds(128 * (2 * h + ih) + i8, 16, stride=8), :] = placed[16 * h : 16 * h + 16, 128 * j : 128 * j + 128]
        own128 = at8(y * 128)
        ypeers(lambda row: push(usend.at[pl.ds(at8(lax.div(row, NZ) * 128 + 8), 112)], urecv.at[pl.ds(at8(own128 + 8), 112)], USUM, a, row))
        urecv[pl.ds(own128, 128), :] = usend[pl.ds(own128, 128), :]

    def sum_terms():
        done(recv, USUM)
        ubuf[8:120, :] = (urecv[8:120, :] + urecv[136:248, :]) + (urecv[264:376, :] + urecv[392:504, :])
        for l in range(1, LEVELS):
            for d in range(1, 2**l):
                at = at8(TOP[l] + lax.rem(flip(a, d), 2**l) * 8)
                push(ubuf.at[pl.ds(at, 8)], lurecv.at[pl.ds(8 * (SLOT[l] + d - 1), 8)], LU + l, flip(a, d), b)

    def form_m0():
        done(recv, AY)
        mbuf[0:16, :] = wcpl[0:16, :] + dot3(split(wcpl[0:16, :]), split(aall[0].reshape(256, 256)))

    def spread(l, value):
        gath[l, pl.ds(own8, 8), :] = value
        mine = gath.at[l, pl.ds(own8, 8)]
        rowpeers(lambda row: push(mine, mine, AG + l, a, row))

    def load_sum(l):
        total = ubuf[pl.ds(at8(TOP[l] + lax.rem(a, 2**l) * 8), 8), :]
        done(recv, LU + l)
        for d in range(1, 2**l):
            total = total + lurecv[8 * (SLOT[l] + d - 1) : 8 * (SLOT[l] + d), :]
        return total

    eye = lax.broadcasted_iota(jnp.int32, (8, 8), 0) == lax.broadcasted_iota(jnp.int32, (8, 8), 1)

    def pivots(l):
        return jnp.sum(jnp.where(eye, jnp.broadcast_to(wpiv[l : l + 1, :], (8, 8)), 0.0), axis=1, keepdims=True)

    def over_leaves(l, sem, rows, first_slot, slots, count):
        for d in range(1, count):
            at = at8(rows + lax.rem(flip(a, d), count) * 8)
            push(part.at[l, pl.ds(at, 8)], slots.at[pl.ds(8 * (first_slot + d - 1), 8)], sem, flip(a, d), b)

    def collect(sem, slots, first_slot, count, total):
        if count > 1:
            done(recv, sem)
            for d in range(1, count):
                total = total + slots[8 * (first_slot + d - 1) : 8 * (first_slot + d), :]
        return total

    def form_m(l):
        n = 2**l
        rows = 2 * n * 8
        done(recv, AY + l)
        own = wcpl[LINK[l] : LINK[l] + rows, :]
        total = own
        for d in range(n):
            if d == 0:
                left = own
            else:
                if l == 2 or d == 1:
                    if not (l == 2 and d == 1):
                        first = 16 if d == 1 else 48
                        done(recv, BX + d)
                at = 96 * (d - 1) + LINK[l] - 16
                left = bpeer[at : at + rows, :]
            block = aall[n - 1 + lax.rem(flip(a, d), n)].reshape(256, 256)
            total = total + dot3(split(left), split(block))
        mbuf[LINK[l] : LINK[l] + rows, :] = total

    def keep_z(l, res, own_part):
        value = collect(YX + l, yrecv, SLOT[l], 2**l, res + own_part)
        value = value / pivots(l)
        at = at8(TOP[l] + lax.rem(a, 2**l) * 8)
        zbuf[pl.ds(at, 8), :] = value
        mine = zbuf.at[pl.ds(at, 8)]
        for d in range(1, 2**l):
            push(mine, mine, ZX + l, flip(a, d), b)
        return value

    below = None
    zs = []
    pending = None
    fetch[7].wait()
    fetch[8].wait()
    for l in range(LEVELS):
        n = 2**l
        if l:
            res = wrhs[l] - load_sum(l) - below
        else:
            done(recv, U0)
            res = wrhs[0] - tree(u0recv)
        spread(l, res)
        if l == 0:
            place_terms()
            done(recv, AZ + 2)
            forward_a(2, 0, 2)
            form_m0()
            for q in range(2):
                m0all[q, b] = mbuf[8 * q : 8 * q + 8, :]
        if l == 1:
            forward_a(2, 2, 2)
        if l == 2:
            zpeers(lambda z2, row: push(m0all.at[:, b], m0all.at[:, b], MZ, a, row))
        if l == 3:
            done(recv, MZ)
            slab0 = m0all.at[:, pl.ds(y * NZ, NZ)]
            ypeers(lambda row: push(slab0, slab0, MY, a, row))
        if l in (1, 2):
            form_m(l)
        if pending is not None:
            zs.append(keep_z(l - 1, *pending))
        lhs = strict[TOP[l] : TOP[l] + 8 * n, :]
        if l < 3:
            lhs = jnp.concatenate([lhs, mbuf[LINK[l] : LINK[l] + 16 * n, :]], axis=0)
        lhs = split(lhs)
        done(recv, AG + l)
        out = dot3(lhs, split(gath[l]))
        part[l, pl.ds(0, out.shape[0]), :] = out
        if l < 3:
            over_leaves(l, PX + l, 8 * n, SLOT[l + 1], precv, 2 * n)
        over_leaves(l, YX + l, 0, SLOT[l], yrecv, n)
        own_y = part[l, pl.ds(at8(lax.rem(a, n) * 8), 8), :]
        if l == 0:
            sum_terms()
        if l < 3:
            below = part[l, pl.ds(at8(8 * n + lax.rem(a, 2 * n) * 8), 8), :]
            below = collect(PX + l, precv, SLOT[l + 1], 2 * n, below)
        pending = (res, own_y)
    zs.append(keep_z(3, *pending))
    z0all[pl.ds(own8, 8), :] = zs[0]
    rowpeers(lambda row: push(z0all.at[pl.ds(own8, 8)], z0all.at[pl.ds(own8, 8)], ZA, a, row))

    def fill(value, first):
        before = [jnp.zeros((first, 128), F32)] if first else []
        after = 128 - first - value.shape[0]
        return split(jnp.concatenate(before + [value] + ([jnp.zeros((after, 128), F32)] if after else []), axis=0))

    def own_half(l):
        n = 2**l
        if l:
            done(recv, ZX + l)
        return dot3(strict_t, fill(zbuf[TOP[l] : TOP[l] + 8 * n, :], TOP[l]))

    def reduce_rows(l, value, total):
        rsend[l] = value
        rrecv[l, pl.ds(own8, 8), :] = rsend[l, pl.ds(own8, 8), :]
        rowpeers(lambda row: push(rsend.at[l, pl.ds(at8(row * 8), 8)], rrecv.at[l, pl.ds(own8, 8)], RS + l, a, row))

    def reduced(l, total):
        done(recv, RS + l)
        return total + tree(rrecv.at[l])

    reduce_rows(3, own_half(3), None)
    m_t = jnp.concatenate([mbuf[0:112, :], jnp.zeros((16, 256), F32)], axis=0)
    m_t = split(jnp.concatenate([m_t[:, :128].T, m_t[:, 128:].T], axis=0))
    done(recv, MY)
    for q in range(4):
        for c in range(2):
            blk = m0all[q // 2, 16 * (q % 2) : 16 * (q % 2) + 16].reshape(128, 256)[:, 128 * c : 128 * c + 128]
            h, lo = split(blk.T)
            m0t_h[128 * c : 128 * c + 128, 128 * q : 128 * q + 128] = h
            m0t_l[128 * c : 128 * c + 128, 128 * q : 128 * q + 128] = lo

    for l in (3, 2, 1):
        n = 2**l
        if l > 1:
            ahead = own_half(l - 1)
        if l == 2:
            done(recv, ZA)
            a0 = aall[0].reshape(256, 256)
            a0 = jnp.concatenate([a0[:, :128].T, a0[:, 128:].T], axis=0)
            c0[...] = z0all[...] + dot3(split(a0), split(z0all[...]))
        if l == 1:
            for m in (2, 3):
                done(recv, PY + m)
            chosen = sel[0:32, 0:32].astype(BF16)
            pieces = []
            for j in range(16):
                ih, i8 = divmod(j, 8)
                pieces.append(jnp.concatenate([xpath[pl.ds(128 * (2 * h + ih) + i8, 16, stride=8), :] for h in range(2)], axis=0))
            pieces = split(jnp.concatenate(pieces, axis=1))
            picked = mm(chosen, pieces[0]) + mm(chosen, pieces[1])
            for j in range(16):
                psend[pl.ds(j, 32, stride=16), :] = picked[:, 128 * j : 128 * j + 128]
            zpeers(lambda z2, row: push(psend.at[pl.ds(at8(z2 * 64), 64)], precv2.at[pl.ds(own64, 64)], PICK, a, row))
            precv2[pl.ds(own64, 64), :] = psend[pl.ds(own64, 64), :]
        value = reduced(l, zs[l])
        at = at8(TOP[l] + lax.rem(a, n) * 8)
        xbuf[pl.ds(at, 8), :] = value
        mine = xbuf.at[pl.ds(at, 8)]
        for d in range(1, n):
            push(mine, mine, XX + l, flip(a, d), b)
        out_win[l] = value
        done(recv, XX + l)
        level = xbuf[TOP[l] : TOP[l] + 8 * n, :]
        if l > 1:
            reduce_rows(l - 1, ahead - dot3(m_t, fill(level, LINK[l - 1])), None)
            block = xbuf.at[pl.ds(TOP[l], 8 * n)]
            there = xpath.at[pl.ds(at8(y * 128 + TOP[l]), 8 * n)]
            ypeers(lambda row: push(block, there, PY + l, a, row))
            xpath[pl.ds(at8(y * 128 + TOP[l]), 8 * n), :] = level
        else:
            for q in range(2):
                x1all[q, b] = level[8 * q : 8 * q + 8]
            rowpeers(lambda row: push(x1all.at[:, b], x1all.at[:, b], X1, a, row))

    done(recv, X1)
    x1 = x1all[...].reshape(512, 128)
    x0all[...] = c0[...] - dot3((m0t_h[...], m0t_l[...]), split(x1))
    out_win[0] = x0all[pl.ds(own8, 8), :]
    tiles = [x0all[0:128, :], x0all[128:256, :]] + [x1[128 * q : 128 * q + 128] for q in range(4)]
    done(recv, PICK)
    rows = []
    for t in range(4):
        for i in range(16):
            ih, z2 = divmod(i, 8)
            at = z2 * 64 + t * 16 + ih * 8
            here = precv2[at : at + 8, :]
            for p in range(6):
                here = here + base[t][p] * tiles[p][8 * i : 8 * i + 8]
            rows.append(here)
    got = split(jnp.concatenate(rows, axis=0))
    for r in range(4):
        s = slice(128 * r, 128 * r + 128)
        yloc[s, :] = zloc[s, :] - dot3((ct_h[s, :], ct_l[s, :]), got)
    after = split(yloc[...])
    for r in range(4):
        s = slice(128 * r, 128 * r + 128)
        k = slice(128 * r, 512)
        out_loc[s, :] = yloc[s, :] + dot3((st_h[s, k], st_l[s, k]), (after[0][k], after[1][k]))

    for sem in views:
        done(send, sem)


def shards(loc_rhs, loc_inverse, loc_coupling, loc_pivots, pattern, win_rhs, win_pivots, win_inverse, win_coupling):
    vmem = pl.BlockSpec(memory_space=pltpu.VMEM)
    specs = [pl.BlockSpec(memory_space=pl.ANY)] * 9
    out_loc, out_win = pl.pallas_call(
        kernel,
        out_shape=(jax.ShapeDtypeStruct((512, 128), F32), jax.ShapeDtypeStruct((LEVELS, 8, 128), F32)),
        in_specs=specs,
        out_specs=(vmem, vmem),
        scratch_shapes=[
            pltpu.VMEM((512, 128), F32),
            pltpu.VMEM((512, 512), F32),
            pltpu.VMEM((512, 512), F32),
            pltpu.VMEM((1, 512), F32),
            pltpu.SMEM((1, 4), jnp.int32),
            pltpu.VMEM((LEVELS, 8, 128), F32),
            pltpu.VMEM((LEVELS, 8), F32),
            pltpu.VMEM((120, 256), F32),
            pltpu.VMEM((112, 256), F32),
            pltpu.VMEM((256, 128), F32),
            pltpu.VMEM((256, 128), F32),
            pltpu.VMEM((256, 128), F32),
            pltpu.VMEM((2, NB, 8, 128), F32),
            pltpu.VMEM((256, 128), F32),
            pltpu.VMEM((256, 128), F32),
            pltpu.VMEM((2, NB, 8, 256), F32),
            pltpu.VMEM((256, 512), BF16),
            pltpu.VMEM((256, 512), BF16),
            pltpu.SemaphoreType.DMA((9,)),
            pltpu.VMEM((512, 512), BF16),
            pltpu.VMEM((512, 512), BF16),
            pltpu.VMEM((512, 512), BF16),
            pltpu.VMEM((512, 512), BF16),
            pltpu.VMEM((512, 128), F32),
            pltpu.VMEM((512, 128), F32),
            pltpu.VMEM((8, 4, 128), F32),
            pltpu.VMEM((128, 128), F32),
            pltpu.VMEM((512, 128), F32),
            pltpu.VMEM((512, 128), F32),
            pltpu.VMEM((512, 128), F32),
            pltpu.VMEM((512, 128), F32),
            pltpu.VMEM((128, 128), F32),
            pltpu.VMEM((88, 128), F32),
            pltpu.VMEM((128, 256), F32),
            pltpu.VMEM((7, NB, 8, 256), F32),
            pltpu.VMEM((288, 256), F32),
            pltpu.VMEM((112, 256), F32),
            pltpu.VMEM((LEVELS, 256, 128), F32),
            pltpu.VMEM((LEVELS, 96, 128), F32),
            pltpu.VMEM((88, 128), F32),
            pltpu.VMEM((88, 128), F32),
            pltpu.VMEM((120, 128), F32),
            pltpu.VMEM((120, 128), F32),
            pltpu.VMEM((LEVELS, 256, 128), F32),
            pltpu.VMEM((LEVELS, 256, 128), F32),
            pltpu.VMEM((512, 128), F32),
            pltpu.VMEM((512, 128), F32),
            pltpu.VMEM((512, 128), F32),
            pltpu.SemaphoreType.DMA((NSEM,)),
            pltpu.SemaphoreType.DMA((NSEM,)),
        ],
        compiler_params=pltpu.CompilerParams(collective_id=0, has_side_effects=True),
    )(
        loc_rhs[0, 0], loc_inverse[0, 0], loc_coupling[0, 0], loc_pivots[0], pattern[0],
        win_rhs, win_pivots, win_inverse[0], win_coupling[0],
    )
    return out_loc[None, None], out_win


def solution(mesh):
    return jax.shard_map(
        shards,
        mesh=mesh,
        in_specs=(
            P("leaf", "row", None, None),
            P("leaf", "row", None, None),
            P("leaf", "row", None, None),
            P("leaf", "row", None),
            P("leaf", "row", None),
            P(None, ("leaf", "row"), None),
            P(None, ("leaf", "row")),
            P("row", None, "leaf"),
            P("row", None, "leaf"),
        ),
        out_specs=(P("leaf", "row", None, None), P(None, ("leaf", "row"), None)),
        check_vma=False,
    )
```

```python
import functools

import jax
import jax.numpy as jnp
from jax import lax
from jax.experimental import pallas as pl
from jax.experimental.pallas import tpu as pltpu
from jax.sharding import PartitionSpec as P

MESH = pl.DeviceIdType.MESH
F32 = jnp.float32
BF16 = jnp.bfloat16
NB, NY, NZ, NA, LEVELS = 32, 4, 8, 8, 4


def split(x):
    hi = x.astype(BF16)
    return hi, (x - hi.astype(F32)).astype(BF16)


def mm(left, right, dims=(((1,), (0,)), ((), ()))):
    return lax.dot_general(left, right, dims, preferred_element_type=F32)


def dot3(left, right):
    (lh, ll), (rh, rl) = left, right
    n = rh.shape[1]
    if n != 128:
        return mm(lh, rh) + (mm(lh, rl) + mm(ll, rh))
    both = mm(lh, jnp.concatenate([rh, rl], axis=1))
    return both[:, :n] + (both[:, n:] + mm(ll, rh))


def flip(a, d):
    out = a
    for k in range(3):
        if (d >> k) & 1:
            out = out + (1 << k) * (1 - 2 * lax.rem(lax.div(a, 1 << k), 2))
    return out


def at8(value):
    return pl.multiple_of(value, 8)


TOP = [(2**l - 1) * 8 for l in range(LEVELS)]
LINK = [(2 * 2**l - 2) * 8 for l in range(LEVELS)]
SLOT = [0, 0, 1, 4]

PAT, TERM, USUM, PICK = 0, 1, 2, 3
AZ, AY, LU, AG, PX, YX, ZX, XX, RS, PY, BX = 4, 7, 10, 14, 18, 22, 26, 30, 34, 38, 42
U0, X1, MZ, MY, ZA = 46, 47, 48, 49, 50
NSEM = 51


def kernel(rhs_in, inv_in, cpl_in, piv_in, pat_in, wrhs_in, wpiv_in, winv_in, wcpl_in, out_loc, out_win,
           rhs, inv, cpl, piv, pat, wrhs, wpiv, winv, wcpl, u0send, u0recv, x0all, x1all, z0all, c0, m0all, m0t_h, m0t_l, loads,
           st_h, st_l, ct_h, ct_l, yloc, zloc, patrecv, sel, tsend, trecv, usend, urecv, ubuf, lurecv,
           strict, aall, bpeer, mbuf, gath, part, precv, yrecv, zbuf, xbuf,
           rsend, rrecv, xpath, psend, precv2, send, recv):
    a = lax.axis_index("leaf")
    b = lax.axis_index("row")
    y = lax.div(b, NZ)
    z = lax.rem(b, NZ)
    own8 = at8(b * 8)

    pairs = [(pat_in, pat), (rhs_in, rhs), (inv_in, inv), (winv_in, winv), (cpl_in, cpl),
             (wcpl_in, wcpl), (piv_in, piv), (wrhs_in, wrhs), (wpiv_in, wpiv)]
    fetch = [pltpu.make_async_copy(src, dst, loads.at[k]) for k, (src, dst) in enumerate(pairs)]
    for copy in fetch:
        copy.start()

    barrier = pltpu.get_barrier_semaphore()

    def greet(d, carry):
        pl.semaphore_signal(barrier, inc=1, device_id=(a, lax.rem(b + d, NB)), device_id_type=MESH)
        return carry

    lax.fori_loop(1, NB, greet, 0)
    for d in range(1, NA):
        pl.semaphore_signal(barrier, inc=1, device_id=(flip(a, d), b), device_id_type=MESH)

    def push(src, dst, sem, leaf, row):
        pltpu.make_async_remote_copy(
            src_ref=src, dst_ref=dst, send_sem=send.at[sem], recv_sem=recv.at[sem],
            device_id=(leaf, row), device_id_type=MESH,
        ).start()

    views = {PAT: patrecv.at[pl.ds(0, 7)], TERM: trecv.at[pl.ds(0, 448)], USUM: urecv.at[pl.ds(0, 336)],
             PICK: precv2.at[pl.ds(0, 448)], U0: u0recv.at[pl.ds(0, 248)],
             X1: x1all.at[:, pl.ds(0, 31)], MZ: m0all.at[:, pl.ds(0, 7)], MY: m0all.at[:, pl.ds(0, 24)],
             ZA: z0all.at[pl.ds(0, 248)]}
    for l in range(LEVELS):
        n = 2**l
        views[AG + l] = gath.at[l, pl.ds(0, 248)]
        if l < 3:
            views[AZ + l] = aall.at[pl.ds(0, n), pl.ds(0, 7)]
            views[AY + l] = aall.at[pl.ds(0, n), pl.ds(0, 24)]
            views[PX + l] = precv.at[pl.ds(0, 8 * (2 * n - 1))]
        if l:
            views[RS + l] = rrecv.at[l, pl.ds(0, 248)]
            views[LU + l] = lurecv.at[pl.ds(0, 8 * (n - 1))]
            views[YX + l] = yrecv.at[pl.ds(0, 8 * (n - 1))]
            views[ZX + l] = zbuf.at[pl.ds(0, 8 * (n - 1))]
            views[XX + l] = xbuf.at[pl.ds(0, 8 * (n - 1))]
        if l > 1:
            views[PY + l] = xpath.at[pl.ds(0, 24 * n)]
    for d in range(1, 4):
        first = 16 if d == 1 else 48
        views[BX + d] = wcpl.at[pl.ds(first, 112 - first)]

    def done(which, sem):
        pltpu.make_async_copy(views[sem], views[sem], which.at[sem]).wait()

    def around(k, n):
        return n // 2 + lax.div(k + 1, 2) * (1 - 2 * lax.rem(k, 2))

    def zpeers(body):
        def step(k, carry):
            z2 = lax.rem(z + around(k, NZ), NZ)
            body(z2, y * NZ + z2)
            return carry

        lax.fori_loop(0, NZ - 1, step, 0)

    def ypeers(body):
        def step(k, carry):
            body(lax.rem(y + around(k, NY), NY) * NZ + z)
            return carry

        lax.fori_loop(0, NY - 1, step, 0)

    def rowpeers(body):
        def step(k, carry):
            y2 = lax.rem(y + around(lax.rem(k, NY), NY), NY)
            z2 = lax.rem(z + around(lax.div(k, NY), NZ), NZ)
            body(y2 * NZ + z2)
            return carry

        lax.fori_loop(0, NB - 1, step, 0)

    sel[...] = jnp.zeros((128, 128), F32)
    xpath[...] = jnp.zeros((512, 128), F32)

    fetch[3].wait()
    for l in range(LEVELS):
        n = 2**l * 8
        rows = lax.broadcasted_iota(jnp.int32, (n, 256), 0)
        cols = lax.broadcasted_iota(jnp.int32, (n, 256), 1)
        row_id = lax.div(rows, 8) * 256 + b * 8 + lax.rem(rows, 8)
        col_id = lax.rem(a, 2**l) * 256 + cols
        block = jnp.where(col_id < row_id, winv[TOP[l] : TOP[l] + n, :], 0.0)
        strict[TOP[l] : TOP[l] + n, :] = block
        if l < 3:
            for q in range(2**l):
                aall[2**l - 1 + q, b] = block[8 * q : 8 * q + 8]
    strict[120:128, :] = jnp.zeros((8, 256), F32)

    fetch[0].wait()
    lane = lax.broadcasted_iota(jnp.int32, (1, 128), 1)
    base = []
    for t in range(4):
        tile = pat[0, t]
        base.append([jnp.where(jnp.full((1, 128), tile, jnp.int32) == p, 1.0, 0.0).astype(F32) for p in range(6)])
        mark = lax.rem(tile, 2) * 16 + lax.div(tile, 2)
        patrecv[z, t : t + 1, :] = jnp.where(lane == mark, 1.0, 0.0).astype(F32)

    pl.semaphore_wait(barrier, NB - 1 + NA - 1)

    zpeers(lambda z2, row: push(patrecv.at[z], patrecv.at[z], PAT, a, row))
    for l in range(2):
        n = 2**l
        zpeers(lambda z2, row: push(aall.at[pl.ds(n - 1, n), b], aall.at[pl.ds(n - 1, n), b], AZ + l, a, row))

    low_row = lax.broadcasted_iota(jnp.int32, (128, 128), 0)
    low_col = lax.broadcasted_iota(jnp.int32, (128, 128), 1)
    low = low_col < low_row
    fetch[1].wait()
    fetch[2].wait()
    right = split(rhs[...])
    for r in range(4):
        acc = rhs[128 * r : 128 * r + 128, :]
        diag = jnp.where(low, inv[128 * r : 128 * r + 128, 128 * r : 128 * r + 128], 0.0)
        acc = acc + dot3(split(diag), (right[0][128 * r : 128 * r + 128], right[1][128 * r : 128 * r + 128]))
        if r:
            acc = acc + dot3(split(inv[128 * r : 128 * r + 128, : 128 * r]), (right[0][: 128 * r], right[1][: 128 * r]))
        yloc[128 * r : 128 * r + 128, :] = acc

    solved = split(yloc[...])
    fetch[4].wait()
    low0, low1 = 0.0, 0.0
    for t in range(4):
        term = dot3(split(cpl[128 * t : 128 * t + 128, :]), solved)
        low0 = low0 + base[t][0] * term
        low1 = low1 + base[t][1] * term
        for i in range(16):
            ih, z2 = divmod(i, 8)
            at = z2 * 64 + t * 16 + ih * 8
            tsend[at : at + 8, :] = term[8 * i : 8 * i + 8]
    u0send[0:128, :] = low0
    u0send[128:256, :] = low1
    rowpeers(lambda row: push(u0send.at[pl.ds(at8(row * 8), 8)], u0recv.at[pl.ds(own8, 8)], U0, a, row))
    u0recv[pl.ds(own8, 8), :] = u0send[pl.ds(own8, 8), :]
    own64 = at8(z * 64)
    zpeers(lambda z2, row: push(tsend.at[pl.ds(at8(z2 * 64), 64)], trecv.at[pl.ds(own64, 64)], TERM, a, row))
    trecv[pl.ds(own64, 64), :] = tsend[pl.ds(own64, 64), :]
    fetch[5].wait()

    for d in range(1, 4):
        first = 16 if d == 1 else 48
        push(wcpl.at[pl.ds(first, 112 - first)], bpeer.at[pl.ds(96 * (d - 1) + first - 16, 112 - first)], BX + d, flip(a, d), b)

    def forward_a(l, first, count):
        slab = aall.at[pl.ds(2**l - 1 + first, count), pl.ds(y * NZ, NZ)]
        ypeers(lambda row: push(slab, slab, AY + l, a, row))

    done(recv, AZ)
    forward_a(0, 0, 1)
    done(recv, AZ + 1)
    forward_a(1, 0, 2)

    for r in range(4):
        for c in range(4):
            blk = cpl[128 * r : 128 * r + 128, 128 * c : 128 * c + 128].T
            h, lo = split(blk)
            ct_h[128 * c : 128 * c + 128, 128 * r : 128 * r + 128] = h
            ct_l[128 * c : 128 * c + 128, 128 * r : 128 * r + 128] = lo
            if c <= r:
                blk = inv[128 * r : 128 * r + 128, 128 * c : 128 * c + 128]
                if c == r:
                    blk = jnp.where(low, blk, 0.0)
                h, lo = split(blk.T)
                st_h[128 * c : 128 * c + 128, 128 * r : 128 * r + 128] = h
                st_l[128 * c : 128 * c + 128, 128 * r : 128 * r + 128] = lo
    strict_t = jnp.concatenate([strict[:, :128].T, strict[:, 128:].T], axis=0)
    strict_t = split(strict_t)
    fetch[6].wait()
    wide = jnp.broadcast_to(piv[...], (128, 512))
    for r in range(4):
        zloc[128 * r : 128 * r + 128, :] = yloc[128 * r : 128 * r + 128, :] / wide[:, 128 * r : 128 * r + 128].T

    def tree(ref):
        sums = [ref[8 * s : 8 * s + 8, :] for s in range(NB)]
        while len(sums) > 1:
            sums = [sums[2 * k] + sums[2 * k + 1] for k in range(len(sums) // 2)]
        return sums[0]

    def place_terms():
        done(recv, PAT)
        for s in range(8):
            sel[4 * s : 4 * s + 4, :] = patrecv[s]
        chosen_t = sel[...].T[:32, :32].astype(BF16)
        done(recv, TERM)
        cols = split(jnp.concatenate([trecv[pl.ds(j, 32, stride=16), :] for j in range(16)], axis=1))
        placed = mm(chosen_t, cols[0]) + mm(chosen_t, cols[1])
        for j in range(16):
            ih, i8 = divmod(j, 8)
            for h in range(2):
                usend[pl.ds(128 * (2 * h + ih) + i8, 16, stride=8), :] = placed[16 * h : 16 * h + 16, 128 * j : 128 * j + 128]
        own128 = at8(y * 128)
        ypeers(lambda row: push(usend.at[pl.ds(at8(lax.div(row, NZ) * 128 + 8), 112)], urecv.at[pl.ds(at8(own128 + 8), 112)], USUM, a, row))
        urecv[pl.ds(own128, 128), :] = usend[pl.ds(own128, 128), :]

    def sum_terms():
        done(recv, USUM)
        ubuf[8:120, :] = (urecv[8:120, :] + urecv[136:248, :]) + (urecv[264:376, :] + urecv[392:504, :])
        for l in range(1, LEVELS):
            for d in range(1, 2**l):
                at = at8(TOP[l] + lax.rem(flip(a, d), 2**l) * 8)
                push(ubuf.at[pl.ds(at, 8)], lurecv.at[pl.ds(8 * (SLOT[l] + d - 1), 8)], LU + l, flip(a, d), b)

    def form_m0():
        done(recv, AY)
        mbuf[0:16, :] = wcpl[0:16, :] + dot3(split(wcpl[0:16, :]), split(aall[0].reshape(256, 256)))

    def spread(l, value):
        gath[l, pl.ds(own8, 8), :] = value
        mine = gath.at[l, pl.ds(own8, 8)]
        rowpeers(lambda row: push(mine, mine, AG + l, a, row))

    def load_sum(l):
        total = ubuf[pl.ds(at8(TOP[l] + lax.rem(a, 2**l) * 8), 8), :]
        done(recv, LU + l)
        for d in range(1, 2**l):
            total = total + lurecv[8 * (SLOT[l] + d - 1) : 8 * (SLOT[l] + d), :]
        return total

    eye = lax.broadcasted_iota(jnp.int32, (8, 8), 0) == lax.broadcasted_iota(jnp.int32, (8, 8), 1)

    def pivots(l):
        return jnp.sum(jnp.where(eye, jnp.broadcast_to(wpiv[l : l + 1, :], (8, 8)), 0.0), axis=1, keepdims=True)

    def over_leaves(l, sem, rows, first_slot, slots, count):
        for d in range(1, count):
            at = at8(rows + lax.rem(flip(a, d), count) * 8)
            push(part.at[l, pl.ds(at, 8)], slots.at[pl.ds(8 * (first_slot + d - 1), 8)], sem, flip(a, d), b)

    def collect(sem, slots, first_slot, count, total):
        if count > 1:
            done(recv, sem)
            for d in range(1, count):
                total = total + slots[8 * (first_slot + d - 1) : 8 * (first_slot + d), :]
        return total

    def form_m(l):
        n = 2**l
        rows = 2 * n * 8
        done(recv, AY + l)
        own = wcpl[LINK[l] : LINK[l] + rows, :]
        total = own
        for d in range(n):
            if d == 0:
                left = own
            else:
                if l == 2 or d == 1:
                    if not (l == 2 and d == 1):
                        first = 16 if d == 1 else 48
                        done(recv, BX + d)
                at = 96 * (d - 1) + LINK[l] - 16
                left = bpeer[at : at + rows, :]
            block = aall[n - 1 + lax.rem(flip(a, d), n)].reshape(256, 256)
            total = total + dot3(split(left), split(block))
        mbuf[LINK[l] : LINK[l] + rows, :] = total

    def keep_z(l, res, own_part):
        value = collect(YX + l, yrecv, SLOT[l], 2**l, res + own_part)
        value = value / pivots(l)
        at = at8(TOP[l] + lax.rem(a, 2**l) * 8)
        zbuf[pl.ds(at, 8), :] = value
        mine = zbuf.at[pl.ds(at, 8)]
        for d in range(1, 2**l):
            push(mine, mine, ZX + l, flip(a, d), b)
        return value

    below = None
    zs = []
    pending = None
    fetch[7].wait()
    fetch[8].wait()
    for l in range(LEVELS):
        n = 2**l
        if l:
            res = wrhs[l] - load_sum(l) - below
        else:
            done(recv, U0)
            res = wrhs[0] - tree(u0recv)
        spread(l, res)
        if l == 0:
            zpeers(lambda z2, row: push(aall.at[pl.ds(3, 4), b], aall.at[pl.ds(3, 4), b], AZ + 2, a, row))
            place_terms()
            form_m0()
            for q in range(2):
                m0all[q, b] = mbuf[8 * q : 8 * q + 8, :]
        if l == 1:
            done(recv, AZ + 2)
            forward_a(2, 0, 4)
        if l == 2:
            zpeers(lambda z2, row: push(m0all.at[:, b], m0all.at[:, b], MZ, a, row))
        if l == 3:
            done(recv, MZ)
            slab0 = m0all.at[:, pl.ds(y * NZ, NZ)]
            ypeers(lambda row: push(slab0, slab0, MY, a, row))
        if l in (1, 2):
            form_m(l)
        if pending is not None:
            zs.append(keep_z(l - 1, *pending))
        lhs = strict[TOP[l] : TOP[l] + 8 * n, :]
        if l < 3:
            lhs = jnp.concatenate([lhs, mbuf[LINK[l] : LINK[l] + 16 * n, :]], axis=0)
        lhs = split(lhs)
        done(recv, AG + l)
        out = dot3(lhs, split(gath[l]))
        part[l, pl.ds(0, out.shape[0]), :] = out
        if l < 3:
            over_leaves(l, PX + l, 8 * n, SLOT[l + 1], precv, 2 * n)
        over_leaves(l, YX + l, 0, SLOT[l], yrecv, n)
        own_y = part[l, pl.ds(at8(lax.rem(a, n) * 8), 8), :]
        if l == 0:
            sum_terms()
        if l < 3:
            below = part[l, pl.ds(at8(8 * n + lax.rem(a, 2 * n) * 8), 8), :]
            below = collect(PX + l, precv, SLOT[l + 1], 2 * n, below)
        pending = (res, own_y)
    zs.append(keep_z(3, *pending))
    z0all[pl.ds(own8, 8), :] = zs[0]
    rowpeers(lambda row: push(z0all.at[pl.ds(own8, 8)], z0all.at[pl.ds(own8, 8)], ZA, a, row))

    def fill(value, first):
        before = [jnp.zeros((first, 128), F32)] if first else []
        after = 128 - first - value.shape[0]
        return split(jnp.concatenate(before + [value] + ([jnp.zeros((after, 128), F32)] if after else []), axis=0))

    def own_half(l):
        n = 2**l
        if l:
            done(recv, ZX + l)
        return dot3(strict_t, fill(zbuf[TOP[l] : TOP[l] + 8 * n, :], TOP[l]))

    def reduce_rows(l, value, total):
        rsend[l] = value
        rrecv[l, pl.ds(own8, 8), :] = rsend[l, pl.ds(own8, 8), :]
        rowpeers(lambda row: push(rsend.at[l, pl.ds(at8(row * 8), 8)], rrecv.at[l, pl.ds(own8, 8)], RS + l, a, row))

    def reduced(l, total):
        done(recv, RS + l)
        return total + tree(rrecv.at[l])

    reduce_rows(3, own_half(3), None)
    m_t = jnp.concatenate([mbuf[0:112, :], jnp.zeros((16, 256), F32)], axis=0)
    m_t = split(jnp.concatenate([m_t[:, :128].T, m_t[:, 128:].T], axis=0))
    done(recv, MY)
    for q in range(4):
        for c in range(2):
            blk = m0all[q // 2, 16 * (q % 2) : 16 * (q % 2) + 16].reshape(128, 256)[:, 128 * c : 128 * c + 128]
            h, lo = split(blk.T)
            m0t_h[128 * c : 128 * c + 128, 128 * q : 128 * q + 128] = h
            m0t_l[128 * c : 128 * c + 128, 128 * q : 128 * q + 128] = lo

    for l in (3, 2, 1):
        n = 2**l
        if l > 1:
            ahead = own_half(l - 1)
        if l == 2:
            done(recv, ZA)
            a0 = aall[0].reshape(256, 256)
            a0 = jnp.concatenate([a0[:, :128].T, a0[:, 128:].T], axis=0)
            c0[...] = z0all[...] + dot3(split(a0), split(z0all[...]))
        if l == 1:
            for m in (2, 3):
                done(recv, PY + m)
            chosen = sel[0:32, 0:32].astype(BF16)
            pieces = []
            for j in range(16):
                ih, i8 = divmod(j, 8)
                pieces.append(jnp.concatenate([xpath[pl.ds(128 * (2 * h + ih) + i8, 16, stride=8), :] for h in range(2)], axis=0))
            pieces = split(jnp.concatenate(pieces, axis=1))
            picked = mm(chosen, pieces[0]) + mm(chosen, pieces[1])
            for j in range(16):
                psend[pl.ds(j, 32, stride=16), :] = picked[:, 128 * j : 128 * j + 128]
            zpeers(lambda z2, row: push(psend.at[pl.ds(at8(z2 * 64), 64)], precv2.at[pl.ds(own64, 64)], PICK, a, row))
            precv2[pl.ds(own64, 64), :] = psend[pl.ds(own64, 64), :]
        value = reduced(l, zs[l])
        at = at8(TOP[l] + lax.rem(a, n) * 8)
        xbuf[pl.ds(at, 8), :] = value
        mine = xbuf.at[pl.ds(at, 8)]
        for d in range(1, n):
            push(mine, mine, XX + l, flip(a, d), b)
        out_win[l] = value
        done(recv, XX + l)
        level = xbuf[TOP[l] : TOP[l] + 8 * n, :]
        if l > 1:
            reduce_rows(l - 1, ahead - dot3(m_t, fill(level, LINK[l - 1])), None)
            block = xbuf.at[pl.ds(TOP[l], 8 * n)]
            there = xpath.at[pl.ds(at8(y * 128 + TOP[l]), 8 * n)]
            ypeers(lambda row: push(block, there, PY + l, a, row))
            xpath[pl.ds(at8(y * 128 + TOP[l]), 8 * n), :] = level
        else:
            for q in range(2):
                x1all[q, b] = level[8 * q : 8 * q + 8]
            rowpeers(lambda row: push(x1all.at[:, b], x1all.at[:, b], X1, a, row))

    done(recv, X1)
    x1 = x1all[...].reshape(512, 128)
    x0all[...] = c0[...] - dot3((m0t_h[...], m0t_l[...]), split(x1))
    out_win[0] = x0all[pl.ds(own8, 8), :]
    tiles = [x0all[0:128, :], x0all[128:256, :]] + [x1[128 * q : 128 * q + 128] for q in range(4)]
    done(recv, PICK)
    rows = []
    for t in range(4):
        for i in range(16):
            ih, z2 = divmod(i, 8)
            at = z2 * 64 + t * 16 + ih * 8
            here = precv2[at : at + 8, :]
            for p in range(6):
                here = here + base[t][p] * tiles[p][8 * i : 8 * i + 8]
            rows.append(here)
    got = split(jnp.concatenate(rows, axis=0))
    for r in range(4):
        s = slice(128 * r, 128 * r + 128)
        yloc[s, :] = zloc[s, :] - dot3((ct_h[s, :], ct_l[s, :]), got)
    after = split(yloc[...])
    for r in range(4):
        s = slice(128 * r, 128 * r + 128)
        k = slice(128 * r, 512)
        out_loc[s, :] = yloc[s, :] + dot3((st_h[s, k], st_l[s, k]), (after[0][k], after[1][k]))

    for sem in views:
        done(send, sem)


def shards(loc_rhs, loc_inverse, loc_coupling, loc_pivots, pattern, win_rhs, win_pivots, win_inverse, win_coupling):
    vmem = pl.BlockSpec(memory_space=pltpu.VMEM)
    specs = [pl.BlockSpec(memory_space=pl.ANY)] * 9
    out_loc, out_win = pl.pallas_call(
        kernel,
        out_shape=(jax.ShapeDtypeStruct((512, 128), F32), jax.ShapeDtypeStruct((LEVELS, 8, 128), F32)),
        in_specs=specs,
        out_specs=(vmem, vmem),
        scratch_shapes=[
            pltpu.VMEM((512, 128), F32),
            pltpu.VMEM((512, 512), F32),
            pltpu.VMEM((512, 512), F32),
            pltpu.VMEM((1, 512), F32),
            pltpu.SMEM((1, 4), jnp.int32),
            pltpu.VMEM((LEVELS, 8, 128), F32),
            pltpu.VMEM((LEVELS, 8), F32),
            pltpu.VMEM((120, 256), F32),
            pltpu.VMEM((112, 256), F32),
            pltpu.VMEM((256, 128), F32),
            pltpu.VMEM((256, 128), F32),
            pltpu.VMEM((256, 128), F32),
            pltpu.VMEM((2, NB, 8, 128), F32),
            pltpu.VMEM((256, 128), F32),
            pltpu.VMEM((256, 128), F32),
            pltpu.VMEM((2, NB, 8, 256), F32),
            pltpu.VMEM((256, 512), BF16),
            pltpu.VMEM((256, 512), BF16),
            pltpu.SemaphoreType.DMA((9,)),
            pltpu.VMEM((512, 512), BF16),
            pltpu.VMEM((512, 512), BF16),
            pltpu.VMEM((512, 512), BF16),
            pltpu.VMEM((512, 512), BF16),
            pltpu.VMEM((512, 128), F32),
            pltpu.VMEM((512, 128), F32),
            pltpu.VMEM((8, 4, 128), F32),
            pltpu.VMEM((128, 128), F32),
            pltpu.VMEM((512, 128), F32),
            pltpu.VMEM((512, 128), F32),
            pltpu.VMEM((512, 128), F32),
            pltpu.VMEM((512, 128), F32),
            pltpu.VMEM((128, 128), F32),
            pltpu.VMEM((88, 128), F32),
            pltpu.VMEM((128, 256), F32),
            pltpu.VMEM((7, NB, 8, 256), F32),
            pltpu.VMEM((288, 256), F32),
            pltpu.VMEM((112, 256), F32),
            pltpu.VMEM((LEVELS, 256, 128), F32),
            pltpu.VMEM((LEVELS, 96, 128), F32),
            pltpu.VMEM((88, 128), F32),
            pltpu.VMEM((88, 128), F32),
            pltpu.VMEM((120, 128), F32),
            pltpu.VMEM((120, 128), F32),
            pltpu.VMEM((LEVELS, 256, 128), F32),
            pltpu.VMEM((LEVELS, 256, 128), F32),
            pltpu.VMEM((512, 128), F32),
            pltpu.VMEM((512, 128), F32),
            pltpu.VMEM((512, 128), F32),
            pltpu.SemaphoreType.DMA((NSEM,)),
            pltpu.SemaphoreType.DMA((NSEM,)),
        ],
        compiler_params=pltpu.CompilerParams(collective_id=0, has_side_effects=True),
    )(
        loc_rhs[0, 0], loc_inverse[0, 0], loc_coupling[0, 0], loc_pivots[0], pattern[0],
        win_rhs, win_pivots, win_inverse[0], win_coupling[0],
    )
    return out_loc[None, None], out_win


def solution(mesh):
    return jax.shard_map(
        shards,
        mesh=mesh,
        in_specs=(
            P("leaf", "row", None, None),
            P("leaf", "row", None, None),
            P("leaf", "row", None, None),
            P("leaf", "row", None),
            P("leaf", "row", None),
            P(None, ("leaf", "row"), None),
            P(None, ("leaf", "row")),
            P("row", None, "leaf"),
            P("row", None, "leaf"),
        ),
        out_specs=(P("leaf", "row", None, None), P(None, ("leaf", "row"), None)),
        check_vma=False,
    )
```

```python
import functools

import jax
import jax.numpy as jnp
from jax import lax
from jax.experimental import pallas as pl
from jax.experimental.pallas import tpu as pltpu
from jax.sharding import PartitionSpec as P

MESH = pl.DeviceIdType.MESH
F32 = jnp.float32
BF16 = jnp.bfloat16
NB, NY, NZ, NA, LEVELS = 32, 4, 8, 8, 4


def split(x):
    hi = x.astype(BF16)
    return hi, (x - hi.astype(F32)).astype(BF16)


def mm(left, right, dims=(((1,), (0,)), ((), ()))):
    return lax.dot_general(left, right, dims, preferred_element_type=F32)


def dot3(left, right):
    (lh, ll), (rh, rl) = left, right
    n = rh.shape[1]
    if n != 128:
        return mm(lh, rh) + (mm(lh, rl) + mm(ll, rh))
    both = mm(lh, jnp.concatenate([rh, rl], axis=1))
    return both[:, :n] + (both[:, n:] + mm(ll, rh))


def flip(a, d):
    out = a
    for k in range(3):
        if (d >> k) & 1:
            out = out + (1 << k) * (1 - 2 * lax.rem(lax.div(a, 1 << k), 2))
    return out


def at8(value):
    return pl.multiple_of(value, 8)


TOP = [(2**l - 1) * 8 for l in range(LEVELS)]
LINK = [(2 * 2**l - 2) * 8 for l in range(LEVELS)]
SLOT = [0, 0, 1, 4]

PAT, TERM, USUM, PICK = 0, 1, 2, 3
AZ, AY, LU, AG, PX, YX, ZX, XX, RS, PY, BX = 4, 7, 10, 14, 18, 22, 26, 30, 34, 38, 42
U0, X1, MZ, MY, ZA, XS = 46, 47, 48, 49, 50, 51
NSEM = 52


def kernel(rhs_in, inv_in, cpl_in, piv_in, pat_in, wrhs_in, wpiv_in, winv_in, wcpl_in, out_loc, out_win,
           rhs, inv, cpl, piv, pat, wrhs, wpiv, winv, wcpl, u0send, u0recv, x0all, x1all, z0all, c0, m0all, m0t_h, m0t_l, loads,
           st_h, st_l, ct_h, ct_l, yloc, zloc, patrecv, sel, tsend, trecv, usend, urecv, ubuf, lurecv,
           strict, aall, bpeer, mbuf, gath, part, precv, yrecv, zbuf, xbuf,
           rsend, rrecv, xpath, psend, precv2, send, recv):
    a = lax.axis_index("leaf")
    b = lax.axis_index("row")
    y = lax.div(b, NZ)
    z = lax.rem(b, NZ)
    own8 = at8(b * 8)

    pairs = [(pat_in, pat), (rhs_in, rhs), (inv_in, inv), (winv_in, winv), (cpl_in, cpl),
             (wcpl_in, wcpl), (piv_in, piv), (wrhs_in, wrhs), (wpiv_in, wpiv)]
    fetch = [pltpu.make_async_copy(src, dst, loads.at[k]) for k, (src, dst) in enumerate(pairs)]
    for copy in fetch:
        copy.start()

    barrier = pltpu.get_barrier_semaphore()

    def greet(d, carry):
        pl.semaphore_signal(barrier, inc=1, device_id=(a, lax.rem(b + d, NB)), device_id_type=MESH)
        return carry

    lax.fori_loop(1, NB, greet, 0)
    for d in range(1, NA):
        pl.semaphore_signal(barrier, inc=1, device_id=(flip(a, d), b), device_id_type=MESH)

    def push(src, dst, sem, leaf, row):
        pltpu.make_async_remote_copy(
            src_ref=src, dst_ref=dst, send_sem=send.at[sem], recv_sem=recv.at[sem],
            device_id=(leaf, row), device_id_type=MESH,
        ).start()

    views = {PAT: patrecv.at[pl.ds(0, 7)], TERM: trecv.at[pl.ds(0, 448)], USUM: urecv.at[pl.ds(0, 336)],
             PICK: precv2.at[pl.ds(0, 448)], U0: u0recv.at[pl.ds(0, 248)],
             X1: x1all.at[0, pl.ds(0, 31)], XS: x1all.at[0], MZ: m0all.at[:, pl.ds(0, 7)], MY: m0all.at[:, pl.ds(0, 24)],
             ZA: z0all.at[pl.ds(0, 248)]}
    for l in range(LEVELS):
        n = 2**l
        views[AG + l] = gath.at[l, pl.ds(0, 248)]
        if l < 3:
            views[AZ + l] = aall.at[pl.ds(0, n), pl.ds(0, 7)]
            views[AY + l] = aall.at[pl.ds(0, n), pl.ds(0, 24)]
            views[PX + l] = precv.at[pl.ds(0, 8 * (2 * n - 1))]
        if l:
            views[RS + l] = rrecv.at[l, pl.ds(0, 248)]
            views[LU + l] = lurecv.at[pl.ds(0, 8 * (n - 1))]
            views[YX + l] = yrecv.at[pl.ds(0, 8 * (n - 1))]
            views[ZX + l] = zbuf.at[pl.ds(0, 8 * (n - 1))]
        if l > 1:
            views[XX + l] = xbuf.at[pl.ds(0, 8 * (n - 1))]
            views[PY + l] = xpath.at[pl.ds(0, 24 * n)]
    for d in range(1, 4):
        first = 16 if d == 1 else 48
        views[BX + d] = wcpl.at[pl.ds(first, 112 - first)]

    def done(which, sem):
        pltpu.make_async_copy(views[sem], views[sem], which.at[sem]).wait()

    def around(k, n):
        return n // 2 + lax.div(k + 1, 2) * (1 - 2 * lax.rem(k, 2))

    def zpeers(body):
        def step(k, carry):
            z2 = lax.rem(z + around(k, NZ), NZ)
            body(z2, y * NZ + z2)
            return carry

        lax.fori_loop(0, NZ - 1, step, 0)

    def ypeers(body):
        def step(k, carry):
            body(lax.rem(y + around(k, NY), NY) * NZ + z)
            return carry

        lax.fori_loop(0, NY - 1, step, 0)

    def rowpeers(body):
        def step(k, carry):
            y2 = lax.rem(y + around(lax.rem(k, NY), NY), NY)
            z2 = lax.rem(z + around(lax.div(k, NY), NZ), NZ)
            body(y2 * NZ + z2)
            return carry

        lax.fori_loop(0, NB - 1, step, 0)

    sel[...] = jnp.zeros((128, 128), F32)
    xpath[...] = jnp.zeros((512, 128), F32)

    fetch[3].wait()
    for l in range(LEVELS):
        n = 2**l * 8
        rows = lax.broadcasted_iota(jnp.int32, (n, 256), 0)
        cols = lax.broadcasted_iota(jnp.int32, (n, 256), 1)
        row_id = lax.div(rows, 8) * 256 + b * 8 + lax.rem(rows, 8)
        col_id = lax.rem(a, 2**l) * 256 + cols
        block = jnp.where(col_id < row_id, winv[TOP[l] : TOP[l] + n, :], 0.0)
        strict[TOP[l] : TOP[l] + n, :] = block
        if l < 3:
            for q in range(2**l):
                aall[2**l - 1 + q, b] = block[8 * q : 8 * q + 8]
    strict[120:128, :] = jnp.zeros((8, 256), F32)

    fetch[0].wait()
    lane = lax.broadcasted_iota(jnp.int32, (1, 128), 1)
    base = []
    for t in range(4):
        tile = pat[0, t]
        base.append([jnp.where(jnp.full((1, 128), tile, jnp.int32) == p, 1.0, 0.0).astype(F32) for p in range(6)])
        mark = lax.rem(tile, 2) * 16 + lax.div(tile, 2)
        patrecv[z, t : t + 1, :] = jnp.where(lane == mark, 1.0, 0.0).astype(F32)

    pl.semaphore_wait(barrier, NB - 1 + NA - 1)

    zpeers(lambda z2, row: push(patrecv.at[z], patrecv.at[z], PAT, a, row))
    for l in range(2):
        n = 2**l
        zpeers(lambda z2, row: push(aall.at[pl.ds(n - 1, n), b], aall.at[pl.ds(n - 1, n), b], AZ + l, a, row))

    low_row = lax.broadcasted_iota(jnp.int32, (128, 128), 0)
    low_col = lax.broadcasted_iota(jnp.int32, (128, 128), 1)
    low = low_col < low_row
    fetch[1].wait()
    fetch[2].wait()
    right = split(rhs[...])
    for r in range(4):
        acc = rhs[128 * r : 128 * r + 128, :]
        diag = jnp.where(low, inv[128 * r : 128 * r + 128, 128 * r : 128 * r + 128], 0.0)
        acc = acc + dot3(split(diag), (right[0][128 * r : 128 * r + 128], right[1][128 * r : 128 * r + 128]))
        if r:
            acc = acc + dot3(split(inv[128 * r : 128 * r + 128, : 128 * r]), (right[0][: 128 * r], right[1][: 128 * r]))
        yloc[128 * r : 128 * r + 128, :] = acc

    solved = split(yloc[...])
    fetch[4].wait()
    low0, low1 = 0.0, 0.0
    for t in range(4):
        term = dot3(split(cpl[128 * t : 128 * t + 128, :]), solved)
        low0 = low0 + base[t][0] * term
        low1 = low1 + base[t][1] * term
        for i in range(16):
            ih, z2 = divmod(i, 8)
            at = z2 * 64 + t * 16 + ih * 8
            tsend[at : at + 8, :] = term[8 * i : 8 * i + 8]
    u0send[0:128, :] = low0
    u0send[128:256, :] = low1
    rowpeers(lambda row: push(u0send.at[pl.ds(at8(row * 8), 8)], u0recv.at[pl.ds(own8, 8)], U0, a, row))
    u0recv[pl.ds(own8, 8), :] = u0send[pl.ds(own8, 8), :]
    own64 = at8(z * 64)
    zpeers(lambda z2, row: push(tsend.at[pl.ds(at8(z2 * 64), 64)], trecv.at[pl.ds(own64, 64)], TERM, a, row))
    trecv[pl.ds(own64, 64), :] = tsend[pl.ds(own64, 64), :]
    fetch[5].wait()

    for d in range(1, 4):
        first = 16 if d == 1 else 48
        push(wcpl.at[pl.ds(first, 112 - first)], bpeer.at[pl.ds(96 * (d - 1) + first - 16, 112 - first)], BX + d, flip(a, d), b)

    def forward_a(l, first, count):
        slab = aall.at[pl.ds(2**l - 1 + first, count), pl.ds(y * NZ, NZ)]
        ypeers(lambda row: push(slab, slab, AY + l, a, row))

    done(recv, AZ)
    forward_a(0, 0, 1)
    done(recv, AZ + 1)
    forward_a(1, 0, 2)

    for r in range(4):
        for c in range(4):
            blk = cpl[128 * r : 128 * r + 128, 128 * c : 128 * c + 128].T
            h, lo = split(blk)
            ct_h[128 * c : 128 * c + 128, 128 * r : 128 * r + 128] = h
            ct_l[128 * c : 128 * c + 128, 128 * r : 128 * r + 128] = lo
            if c <= r:
                blk = inv[128 * r : 128 * r + 128, 128 * c : 128 * c + 128]
                if c == r:
                    blk = jnp.where(low, blk, 0.0)
                h, lo = split(blk.T)
                st_h[128 * c : 128 * c + 128, 128 * r : 128 * r + 128] = h
                st_l[128 * c : 128 * c + 128, 128 * r : 128 * r + 128] = lo
    strict_t = jnp.concatenate([strict[:, :128].T, strict[:, 128:].T], axis=0)
    strict_t = split(strict_t)
    fetch[6].wait()
    wide = jnp.broadcast_to(piv[...], (128, 512))
    for r in range(4):
        zloc[128 * r : 128 * r + 128, :] = yloc[128 * r : 128 * r + 128, :] / wide[:, 128 * r : 128 * r + 128].T

    def tree(ref):
        sums = [ref[8 * s : 8 * s + 8, :] for s in range(NB)]
        while len(sums) > 1:
            sums = [sums[2 * k] + sums[2 * k + 1] for k in range(len(sums) // 2)]
        return sums[0]

    def place_terms():
        done(recv, PAT)
        for s in range(8):
            sel[4 * s : 4 * s + 4, :] = patrecv[s]
        chosen_t = sel[...].T[:32, :32].astype(BF16)
        done(recv, TERM)
        cols = split(jnp.concatenate([trecv[pl.ds(j, 32, stride=16), :] for j in range(16)], axis=1))
        placed = mm(chosen_t, cols[0]) + mm(chosen_t, cols[1])
        for j in range(16):
            ih, i8 = divmod(j, 8)
            for h in range(2):
                usend[pl.ds(128 * (2 * h + ih) + i8, 16, stride=8), :] = placed[16 * h : 16 * h + 16, 128 * j : 128 * j + 128]
        own128 = at8(y * 128)
        ypeers(lambda row: push(usend.at[pl.ds(at8(lax.div(row, NZ) * 128 + 8), 112)], urecv.at[pl.ds(at8(own128 + 8), 112)], USUM, a, row))
        urecv[pl.ds(own128, 128), :] = usend[pl.ds(own128, 128), :]

    def sum_terms():
        done(recv, USUM)
        ubuf[8:120, :] = (urecv[8:120, :] + urecv[136:248, :]) + (urecv[264:376, :] + urecv[392:504, :])
        for l in range(1, LEVELS):
            for d in range(1, 2**l):
                at = at8(TOP[l] + lax.rem(flip(a, d), 2**l) * 8)
                push(ubuf.at[pl.ds(at, 8)], lurecv.at[pl.ds(8 * (SLOT[l] + d - 1), 8)], LU + l, flip(a, d), b)

    def form_m0():
        done(recv, AY)
        mbuf[0:16, :] = wcpl[0:16, :] + dot3(split(wcpl[0:16, :]), split(aall[0].reshape(256, 256)))

    def spread(l, value):
        gath[l, pl.ds(own8, 8), :] = value
        mine = gath.at[l, pl.ds(own8, 8)]
        rowpeers(lambda row: push(mine, mine, AG + l, a, row))

    def load_sum(l):
        total = ubuf[pl.ds(at8(TOP[l] + lax.rem(a, 2**l) * 8), 8), :]
        done(recv, LU + l)
        for d in range(1, 2**l):
            total = total + lurecv[8 * (SLOT[l] + d - 1) : 8 * (SLOT[l] + d), :]
        return total

    eye = lax.broadcasted_iota(jnp.int32, (8, 8), 0) == lax.broadcasted_iota(jnp.int32, (8, 8), 1)

    def pivots(l):
        return jnp.sum(jnp.where(eye, jnp.broadcast_to(wpiv[l : l + 1, :], (8, 8)), 0.0), axis=1, keepdims=True)

    def over_leaves(l, sem, rows, first_slot, slots, count):
        for d in range(1, count):
            at = at8(rows + lax.rem(flip(a, d), count) * 8)
            push(part.at[l, pl.ds(at, 8)], slots.at[pl.ds(8 * (first_slot + d - 1), 8)], sem, flip(a, d), b)

    def collect(sem, slots, first_slot, count, total):
        if count > 1:
            done(recv, sem)
            for d in range(1, count):
                total = total + slots[8 * (first_slot + d - 1) : 8 * (first_slot + d), :]
        return total

    def form_m(l):
        n = 2**l
        rows = 2 * n * 8
        done(recv, AY + l)
        own = wcpl[LINK[l] : LINK[l] + rows, :]
        total = own
        for d in range(n):
            if d == 0:
                left = own
            else:
                if l == 2 or d == 1:
                    if not (l == 2 and d == 1):
                        first = 16 if d == 1 else 48
                        done(recv, BX + d)
                at = 96 * (d - 1) + LINK[l] - 16
                left = bpeer[at : at + rows, :]
            block = aall[n - 1 + lax.rem(flip(a, d), n)].reshape(256, 256)
            total = total + dot3(split(left), split(block))
        mbuf[LINK[l] : LINK[l] + rows, :] = total

    def keep_z(l, res, own_part):
        value = collect(YX + l, yrecv, SLOT[l], 2**l, res + own_part)
        value = value / pivots(l)
        at = at8(TOP[l] + lax.rem(a, 2**l) * 8)
        zbuf[pl.ds(at, 8), :] = value
        mine = zbuf.at[pl.ds(at, 8)]
        for d in range(1, 2**l):
            push(mine, mine, ZX + l, flip(a, d), b)
        return value

    below = None
    zs = []
    pending = None
    fetch[7].wait()
    fetch[8].wait()
    for l in range(LEVELS):
        n = 2**l
        if l:
            res = wrhs[l] - load_sum(l) - below
        else:
            done(recv, U0)
            res = wrhs[0] - tree(u0recv)
        spread(l, res)
        if l == 0:
            zpeers(lambda z2, row: push(aall.at[pl.ds(3, 4), b], aall.at[pl.ds(3, 4), b], AZ + 2, a, row))
            place_terms()
            form_m0()
            for q in range(2):
                m0all[q, b] = mbuf[8 * q : 8 * q + 8, :]
        if l == 1:
            done(recv, AZ + 2)
            forward_a(2, 0, 4)
        if l == 2:
            zpeers(lambda z2, row: push(m0all.at[:, b], m0all.at[:, b], MZ, a, row))
        if l == 3:
            done(recv, MZ)
            slab0 = m0all.at[:, pl.ds(y * NZ, NZ)]
            ypeers(lambda row: push(slab0, slab0, MY, a, row))
        if l in (1, 2):
            form_m(l)
        if pending is not None:
            zs.append(keep_z(l - 1, *pending))
        lhs = strict[TOP[l] : TOP[l] + 8 * n, :]
        if l < 3:
            lhs = jnp.concatenate([lhs, mbuf[LINK[l] : LINK[l] + 16 * n, :]], axis=0)
        lhs = split(lhs)
        done(recv, AG + l)
        out = dot3(lhs, split(gath[l]))
        part[l, pl.ds(0, out.shape[0]), :] = out
        if l < 3:
            over_leaves(l, PX + l, 8 * n, SLOT[l + 1], precv, 2 * n)
        over_leaves(l, YX + l, 0, SLOT[l], yrecv, n)
        own_y = part[l, pl.ds(at8(lax.rem(a, n) * 8), 8), :]
        if l == 0:
            sum_terms()
        if l < 3:
            below = part[l, pl.ds(at8(8 * n + lax.rem(a, 2 * n) * 8), 8), :]
            below = collect(PX + l, precv, SLOT[l + 1], 2 * n, below)
        pending = (res, own_y)
    zs.append(keep_z(3, *pending))
    z0all[pl.ds(own8, 8), :] = zs[0]
    rowpeers(lambda row: push(z0all.at[pl.ds(own8, 8)], z0all.at[pl.ds(own8, 8)], ZA, a, row))

    def fill(value, first):
        before = [jnp.zeros((first, 128), F32)] if first else []
        after = 128 - first - value.shape[0]
        return split(jnp.concatenate(before + [value] + ([jnp.zeros((after, 128), F32)] if after else []), axis=0))

    def own_half(l):
        n = 2**l
        if l:
            done(recv, ZX + l)
        return dot3(strict_t, fill(zbuf[TOP[l] : TOP[l] + 8 * n, :], TOP[l]))

    def reduce_rows(l, value, total):
        rsend[l] = value
        rrecv[l, pl.ds(own8, 8), :] = rsend[l, pl.ds(own8, 8), :]
        rowpeers(lambda row: push(rsend.at[l, pl.ds(at8(row * 8), 8)], rrecv.at[l, pl.ds(own8, 8)], RS + l, a, row))

    def reduced(l, total):
        done(recv, RS + l)
        return total + tree(rrecv.at[l])

    reduce_rows(3, own_half(3), None)
    m_t = jnp.concatenate([mbuf[0:112, :], jnp.zeros((16, 256), F32)], axis=0)
    m_t = split(jnp.concatenate([m_t[:, :128].T, m_t[:, 128:].T], axis=0))
    done(recv, MY)
    for q in range(4):
        for c in range(2):
            blk = m0all[q // 2, 16 * (q % 2) : 16 * (q % 2) + 16].reshape(128, 256)[:, 128 * c : 128 * c + 128]
            h, lo = split(blk.T)
            m0t_h[128 * c : 128 * c + 128, 128 * q : 128 * q + 128] = h
            m0t_l[128 * c : 128 * c + 128, 128 * q : 128 * q + 128] = lo

    for l in (3, 2, 1):
        n = 2**l
        if l > 1:
            ahead = own_half(l - 1)
        if l == 2:
            done(recv, ZA)
            a0 = aall[0].reshape(256, 256)
            a0 = jnp.concatenate([a0[:, :128].T, a0[:, 128:].T], axis=0)
            c0[...] = z0all[...] + dot3(split(a0), split(z0all[...]))
        if l == 1:
            for m in (2, 3):
                done(recv, PY + m)
            chosen = sel[0:32, 0:32].astype(BF16)
            pieces = []
            for j in range(16):
                ih, i8 = divmod(j, 8)
                pieces.append(jnp.concatenate([xpath[pl.ds(128 * (2 * h + ih) + i8, 16, stride=8), :] for h in range(2)], axis=0))
            pieces = split(jnp.concatenate(pieces, axis=1))
            picked = mm(chosen, pieces[0]) + mm(chosen, pieces[1])
            for j in range(16):
                psend[pl.ds(j, 32, stride=16), :] = picked[:, 128 * j : 128 * j + 128]
            precv2[pl.ds(own64, 64), :] = psend[pl.ds(own64, 64), :]
        value = reduced(l, zs[l])
        if l > 1:
            at = at8(TOP[l] + lax.rem(a, n) * 8)
            xbuf[pl.ds(at, 8), :] = value
            mine = xbuf.at[pl.ds(at, 8)]
            for d in range(1, n):
                push(mine, mine, XX + l, flip(a, d), b)
            out_win[l] = value
            done(recv, XX + l)
            level = xbuf[TOP[l] : TOP[l] + 8 * n, :]
            reduce_rows(l - 1, ahead - dot3(m_t, fill(level, LINK[l - 1])), None)
            block = xbuf.at[pl.ds(TOP[l], 8 * n)]
            there = xpath.at[pl.ds(at8(y * 128 + TOP[l]), 8 * n)]
            ypeers(lambda row: push(block, there, PY + l, a, row))
            xpath[pl.ds(at8(y * 128 + TOP[l]), 8 * n), :] = level
        else:
            half = lax.rem(a, 2)
            x1all[half, b] = value
            rowpeers(lambda row: push(x1all.at[half, b], x1all.at[half, b], X1, a, row))
            zpeers(lambda z2, row: push(psend.at[pl.ds(at8(z2 * 64), 64)], precv2.at[pl.ds(own64, 64)], PICK, a, row))
            out_win[l] = value

    done(recv, X1)
    push(x1all.at[half], x1all.at[half], XS, flip(a, 1), b)
    done(recv, XS)
    x1 = x1all[...].reshape(512, 128)
    x0all[...] = c0[...] - dot3((m0t_h[...], m0t_l[...]), split(x1))
    out_win[0] = x0all[pl.ds(own8, 8), :]
    tiles = [x0all[0:128, :], x0all[128:256, :]] + [x1[128 * q : 128 * q + 128] for q in range(4)]
    done(recv, PICK)
    rows = []
    for t in range(4):
        for i in range(16):
            ih, z2 = divmod(i, 8)
            at = z2 * 64 + t * 16 + ih * 8
            here = precv2[at : at + 8, :]
            for p in range(6):
                here = here + base[t][p] * tiles[p][8 * i : 8 * i + 8]
            rows.append(here)
    got = split(jnp.concatenate(rows, axis=0))
    for r in range(4):
        s = slice(128 * r, 128 * r + 128)
        yloc[s, :] = zloc[s, :] - dot3((ct_h[s, :], ct_l[s, :]), got)
    after = split(yloc[...])
    for r in range(4):
        s = slice(128 * r, 128 * r + 128)
        k = slice(128 * r, 512)
        out_loc[s, :] = yloc[s, :] + dot3((st_h[s, k], st_l[s, k]), (after[0][k], after[1][k]))

    for sem in views:
        done(send, sem)


def shards(loc_rhs, loc_inverse, loc_coupling, loc_pivots, pattern, win_rhs, win_pivots, win_inverse, win_coupling):
    vmem = pl.BlockSpec(memory_space=pltpu.VMEM)
    specs = [pl.BlockSpec(memory_space=pl.ANY)] * 9
    out_loc, out_win = pl.pallas_call(
        kernel,
        out_shape=(jax.ShapeDtypeStruct((512, 128), F32), jax.ShapeDtypeStruct((LEVELS, 8, 128), F32)),
        in_specs=specs,
        out_specs=(vmem, vmem),
        scratch_shapes=[
            pltpu.VMEM((512, 128), F32),
            pltpu.VMEM((512, 512), F32),
            pltpu.VMEM((512, 512), F32),
            pltpu.VMEM((1, 512), F32),
            pltpu.SMEM((1, 4), jnp.int32),
            pltpu.VMEM((LEVELS, 8, 128), F32),
            pltpu.VMEM((LEVELS, 8), F32),
            pltpu.VMEM((120, 256), F32),
            pltpu.VMEM((112, 256), F32),
            pltpu.VMEM((256, 128), F32),
            pltpu.VMEM((256, 128), F32),
            pltpu.VMEM((256, 128), F32),
            pltpu.VMEM((2, NB, 8, 128), F32),
            pltpu.VMEM((256, 128), F32),
            pltpu.VMEM((256, 128), F32),
            pltpu.VMEM((2, NB, 8, 256), F32),
            pltpu.VMEM((256, 512), BF16),
            pltpu.VMEM((256, 512), BF16),
            pltpu.SemaphoreType.DMA((9,)),
            pltpu.VMEM((512, 512), BF16),
            pltpu.VMEM((512, 512), BF16),
            pltpu.VMEM((512, 512), BF16),
            pltpu.VMEM((512, 512), BF16),
            pltpu.VMEM((512, 128), F32),
            pltpu.VMEM((512, 128), F32),
            pltpu.VMEM((8, 4, 128), F32),
            pltpu.VMEM((128, 128), F32),
            pltpu.VMEM((512, 128), F32),
            pltpu.VMEM((512, 128), F32),
            pltpu.VMEM((512, 128), F32),
            pltpu.VMEM((512, 128), F32),
            pltpu.VMEM((128, 128), F32),
            pltpu.VMEM((88, 128), F32),
            pltpu.VMEM((128, 256), F32),
            pltpu.VMEM((7, NB, 8, 256), F32),
            pltpu.VMEM((288, 256), F32),
            pltpu.VMEM((112, 256), F32),
            pltpu.VMEM((LEVELS, 256, 128), F32),
            pltpu.VMEM((LEVELS, 96, 128), F32),
            pltpu.VMEM((88, 128), F32),
            pltpu.VMEM((88, 128), F32),
            pltpu.VMEM((120, 128), F32),
            pltpu.VMEM((120, 128), F32),
            pltpu.VMEM((LEVELS, 256, 128), F32),
            pltpu.VMEM((LEVELS, 256, 128), F32),
            pltpu.VMEM((512, 128), F32),
            pltpu.VMEM((512, 128), F32),
            pltpu.VMEM((512, 128), F32),
            pltpu.SemaphoreType.DMA((NSEM,)),
            pltpu.SemaphoreType.DMA((NSEM,)),
        ],
        compiler_params=pltpu.CompilerParams(collective_id=0, has_side_effects=True),
    )(
        loc_rhs[0, 0], loc_inverse[0, 0], loc_coupling[0, 0], loc_pivots[0], pattern[0],
        win_rhs, win_pivots, win_inverse[0], win_coupling[0],
    )
    return out_loc[None, None], out_win


def solution(mesh):
    return jax.shard_map(
        shards,
        mesh=mesh,
        in_specs=(
            P("leaf", "row", None, None),
            P("leaf", "row", None, None),
            P("leaf", "row", None, None),
            P("leaf", "row", None),
            P("leaf", "row", None),
            P(None, ("leaf", "row"), None),
            P(None, ("leaf", "row")),
            P("row", None, "leaf"),
            P("row", None, "leaf"),
        ),
        out_specs=(P("leaf", "row", None, None), P(None, ("leaf", "row"), None)),
        check_vma=False,
    )
```

```python
import functools

import jax
import jax.numpy as jnp
from jax import lax
from jax.experimental import pallas as pl
from jax.experimental.pallas import tpu as pltpu
from jax.sharding import PartitionSpec as P

MESH = pl.DeviceIdType.MESH
F32 = jnp.float32
BF16 = jnp.bfloat16
NB, NY, NZ, NA, LEVELS = 32, 4, 8, 8, 4


def split(x):
    hi = x.astype(BF16)
    return hi, (x - hi.astype(F32)).astype(BF16)


def mm(left, right, dims=(((1,), (0,)), ((), ()))):
    return lax.dot_general(left, right, dims, preferred_element_type=F32)


def dot3(left, right):
    (lh, ll), (rh, rl) = left, right
    n = rh.shape[1]
    if n != 128:
        return mm(lh, rh) + (mm(lh, rl) + mm(ll, rh))
    both = mm(lh, jnp.concatenate([rh, rl], axis=1))
    return both[:, :n] + (both[:, n:] + mm(ll, rh))


def flip(a, d):
    out = a
    for k in range(3):
        if (d >> k) & 1:
            out = out + (1 << k) * (1 - 2 * lax.rem(lax.div(a, 1 << k), 2))
    return out


def at8(value):
    return pl.multiple_of(value, 8)


TOP = [(2**l - 1) * 8 for l in range(LEVELS)]
LINK = [(2 * 2**l - 2) * 8 for l in range(LEVELS)]
SLOT = [0, 0, 1, 4]

PAT, TERM, USUM, PICK = 0, 1, 2, 3
AZ, AY, LU, AG, PX, YX, ZX, XX, RS, PY, BX = 4, 7, 10, 14, 18, 22, 26, 30, 34, 38, 42
U0, X1, MZ, MY, ZA, XS = 46, 47, 48, 49, 50, 51
NSEM = 52


def kernel(rhs_in, inv_in, cpl_in, piv_in, pat_in, wrhs_in, wpiv_in, winv_in, wcpl_in, out_loc, out_win,
           rhs, inv, cpl, piv, pat, wrhs, wpiv, winv, wcpl, u0send, u0recv, x0all, x1all, z0all, c0, m0all, m0t_h, m0t_l, loads,
           st_h, st_l, ct_h, ct_l, yloc, zloc, patrecv, sel, tsend, trecv, usend, urecv, ubuf, lurecv,
           strict, aall, bpeer, mbuf, gath, part, precv, yrecv, zbuf, xbuf,
           rsend, rrecv, xpath, psend, precv2, send, recv):
    a = lax.axis_index("leaf")
    b = lax.axis_index("row")
    y = lax.div(b, NZ)
    z = lax.rem(b, NZ)
    own8 = at8(b * 8)

    pairs = [(pat_in, pat), (rhs_in, rhs), (inv_in, inv), (winv_in, winv), (cpl_in, cpl),
             (wcpl_in, wcpl), (piv_in, piv), (wrhs_in, wrhs), (wpiv_in, wpiv)]
    fetch = [pltpu.make_async_copy(src, dst, loads.at[k]) for k, (src, dst) in enumerate(pairs)]
    for copy in fetch:
        copy.start()

    barrier = pltpu.get_barrier_semaphore()

    def greet(d, carry):
        pl.semaphore_signal(barrier, inc=1, device_id=(a, lax.rem(b + d, NB)), device_id_type=MESH)
        return carry

    lax.fori_loop(1, NB, greet, 0)
    for d in range(1, NA):
        pl.semaphore_signal(barrier, inc=1, device_id=(flip(a, d), b), device_id_type=MESH)

    def push(src, dst, sem, leaf, row):
        pltpu.make_async_remote_copy(
            src_ref=src, dst_ref=dst, send_sem=send.at[sem], recv_sem=recv.at[sem],
            device_id=(leaf, row), device_id_type=MESH,
        ).start()

    views = {PAT: patrecv.at[pl.ds(0, 7)], TERM: trecv.at[pl.ds(0, 448)], USUM: urecv.at[pl.ds(0, 336)],
             PICK: precv2.at[pl.ds(0, 448)], U0: u0recv.at[pl.ds(0, 248)],
             X1: x1all.at[0, pl.ds(0, 31)], XS: x1all.at[0], MZ: m0all.at[:, pl.ds(0, 7)], MY: m0all.at[:, pl.ds(0, 24)],
             ZA: z0all.at[pl.ds(0, 248)]}
    for l in range(LEVELS):
        n = 2**l
        views[AG + l] = gath.at[l, pl.ds(0, 248)]
        if l < 3:
            views[AZ + l] = aall.at[pl.ds(0, n), pl.ds(0, 7)]
            views[AY + l] = aall.at[pl.ds(0, n), pl.ds(0, 24)]
            views[PX + l] = precv.at[pl.ds(0, 8 * (2 * n - 1))]
        if l:
            views[RS + l] = rrecv.at[l, pl.ds(0, 248)]
            views[LU + l] = lurecv.at[pl.ds(0, 8 * (n - 1))]
            views[YX + l] = yrecv.at[pl.ds(0, 8 * (n - 1))]
            views[ZX + l] = zbuf.at[pl.ds(0, 8 * (n - 1))]
        if l > 1:
            views[XX + l] = xbuf.at[pl.ds(0, 8 * (n - 1))]
            views[PY + l] = xpath.at[pl.ds(0, 24 * n)]
    for d in range(1, 4):
        first = 16 if d == 1 else 48
        views[BX + d] = wcpl.at[pl.ds(first, 112 - first)]

    def done(which, sem):
        pltpu.make_async_copy(views[sem], views[sem], which.at[sem]).wait()

    def around(k, n):
        return n // 2 + lax.div(k + 1, 2) * (1 - 2 * lax.rem(k, 2))

    def zpeers(body):
        def step(k, carry):
            z2 = lax.rem(z + around(k, NZ), NZ)
            body(z2, y * NZ + z2)
            return carry

        lax.fori_loop(0, NZ - 1, step, 0)

    def ypeers(body):
        def step(k, carry):
            body(lax.rem(y + around(k, NY), NY) * NZ + z)
            return carry

        lax.fori_loop(0, NY - 1, step, 0)

    ring_y = [lax.rem(y + d, NY) * NZ for d in (2, 1, 3, 0)]

    def rowpeers(body):
        def step(k, carry):
            z2 = lax.rem(z + around(k, NZ), NZ)
            for y2 in ring_y:
                body(y2 + z2)
            return carry

        lax.fori_loop(0, NZ - 1, step, 0)
        for y2 in ring_y[:-1]:
            body(y2 + z)

    sel[...] = jnp.zeros((128, 128), F32)
    xpath[...] = jnp.zeros((512, 128), F32)

    fetch[3].wait()
    for l in range(LEVELS):
        n = 2**l * 8
        rows = lax.broadcasted_iota(jnp.int32, (n, 256), 0)
        cols = lax.broadcasted_iota(jnp.int32, (n, 256), 1)
        row_id = lax.div(rows, 8) * 256 + b * 8 + lax.rem(rows, 8)
        col_id = lax.rem(a, 2**l) * 256 + cols
        block = jnp.where(col_id < row_id, winv[TOP[l] : TOP[l] + n, :], 0.0)
        strict[TOP[l] : TOP[l] + n, :] = block
        if l < 3:
            for q in range(2**l):
                aall[2**l - 1 + q, b] = block[8 * q : 8 * q + 8]
    strict[120:128, :] = jnp.zeros((8, 256), F32)

    fetch[0].wait()
    lane = lax.broadcasted_iota(jnp.int32, (1, 128), 1)
    base = []
    for t in range(4):
        tile = pat[0, t]
        base.append([jnp.where(jnp.full((1, 128), tile, jnp.int32) == p, 1.0, 0.0).astype(F32) for p in range(6)])
        mark = lax.rem(tile, 2) * 16 + lax.div(tile, 2)
        patrecv[z, t : t + 1, :] = jnp.where(lane == mark, 1.0, 0.0).astype(F32)

    pl.semaphore_wait(barrier, NB - 1 + NA - 1)

    zpeers(lambda z2, row: push(patrecv.at[z], patrecv.at[z], PAT, a, row))
    for l in range(2):
        n = 2**l
        zpeers(lambda z2, row: push(aall.at[pl.ds(n - 1, n), b], aall.at[pl.ds(n - 1, n), b], AZ + l, a, row))

    low_row = lax.broadcasted_iota(jnp.int32, (128, 128), 0)
    low_col = lax.broadcasted_iota(jnp.int32, (128, 128), 1)
    low = low_col < low_row
    fetch[1].wait()
    fetch[2].wait()
    right = split(rhs[...])
    for r in range(4):
        acc = rhs[128 * r : 128 * r + 128, :]
        diag = jnp.where(low, inv[128 * r : 128 * r + 128, 128 * r : 128 * r + 128], 0.0)
        acc = acc + dot3(split(diag), (right[0][128 * r : 128 * r + 128], right[1][128 * r : 128 * r + 128]))
        if r:
            acc = acc + dot3(split(inv[128 * r : 128 * r + 128, : 128 * r]), (right[0][: 128 * r], right[1][: 128 * r]))
        yloc[128 * r : 128 * r + 128, :] = acc

    solved = split(yloc[...])
    fetch[4].wait()
    low0, low1 = 0.0, 0.0
    for t in range(4):
        term = dot3(split(cpl[128 * t : 128 * t + 128, :]), solved)
        low0 = low0 + base[t][0] * term
        low1 = low1 + base[t][1] * term
        for i in range(16):
            ih, z2 = divmod(i, 8)
            at = z2 * 64 + t * 16 + ih * 8
            tsend[at : at + 8, :] = term[8 * i : 8 * i + 8]
    u0send[0:128, :] = low0
    u0send[128:256, :] = low1
    rowpeers(lambda row: push(u0send.at[pl.ds(at8(row * 8), 8)], u0recv.at[pl.ds(own8, 8)], U0, a, row))
    u0recv[pl.ds(own8, 8), :] = u0send[pl.ds(own8, 8), :]
    own64 = at8(z * 64)
    zpeers(lambda z2, row: push(tsend.at[pl.ds(at8(z2 * 64), 64)], trecv.at[pl.ds(own64, 64)], TERM, a, row))
    trecv[pl.ds(own64, 64), :] = tsend[pl.ds(own64, 64), :]
    fetch[5].wait()

    for d in range(1, 4):
        first = 16 if d == 1 else 48
        push(wcpl.at[pl.ds(first, 112 - first)], bpeer.at[pl.ds(96 * (d - 1) + first - 16, 112 - first)], BX + d, flip(a, d), b)

    def forward_a(l, first, count):
        slab = aall.at[pl.ds(2**l - 1 + first, count), pl.ds(y * NZ, NZ)]
        ypeers(lambda row: push(slab, slab, AY + l, a, row))

    done(recv, AZ)
    forward_a(0, 0, 1)
    done(recv, AZ + 1)
    forward_a(1, 0, 2)

    for r in range(4):
        for c in range(4):
            blk = cpl[128 * r : 128 * r + 128, 128 * c : 128 * c + 128].T
            h, lo = split(blk)
            ct_h[128 * c : 128 * c + 128, 128 * r : 128 * r + 128] = h
            ct_l[128 * c : 128 * c + 128, 128 * r : 128 * r + 128] = lo
            if c <= r:
                blk = inv[128 * r : 128 * r + 128, 128 * c : 128 * c + 128]
                if c == r:
                    blk = jnp.where(low, blk, 0.0)
                h, lo = split(blk.T)
                st_h[128 * c : 128 * c + 128, 128 * r : 128 * r + 128] = h
                st_l[128 * c : 128 * c + 128, 128 * r : 128 * r + 128] = lo
    strict_t = jnp.concatenate([strict[:, :128].T, strict[:, 128:].T], axis=0)
    strict_t = split(strict_t)
    fetch[6].wait()
    wide = jnp.broadcast_to(piv[...], (128, 512))
    for r in range(4):
        zloc[128 * r : 128 * r + 128, :] = yloc[128 * r : 128 * r + 128, :] / wide[:, 128 * r : 128 * r + 128].T

    def tree(ref):
        sums = [ref[8 * s : 8 * s + 8, :] for s in range(NB)]
        while len(sums) > 1:
            sums = [sums[2 * k] + sums[2 * k + 1] for k in range(len(sums) // 2)]
        return sums[0]

    def place_terms():
        done(recv, PAT)
        for s in range(8):
            sel[4 * s : 4 * s + 4, :] = patrecv[s]
        chosen_t = sel[...].T[:32, :32].astype(BF16)
        done(recv, TERM)
        cols = split(jnp.concatenate([trecv[pl.ds(j, 32, stride=16), :] for j in range(16)], axis=1))
        placed = mm(chosen_t, cols[0]) + mm(chosen_t, cols[1])
        for j in range(16):
            ih, i8 = divmod(j, 8)
            for h in range(2):
                usend[pl.ds(128 * (2 * h + ih) + i8, 16, stride=8), :] = placed[16 * h : 16 * h + 16, 128 * j : 128 * j + 128]
        own128 = at8(y * 128)
        ypeers(lambda row: push(usend.at[pl.ds(at8(lax.div(row, NZ) * 128 + 8), 112)], urecv.at[pl.ds(at8(own128 + 8), 112)], USUM, a, row))
        urecv[pl.ds(own128, 128), :] = usend[pl.ds(own128, 128), :]

    def sum_terms():
        done(recv, USUM)
        ubuf[8:120, :] = (urecv[8:120, :] + urecv[136:248, :]) + (urecv[264:376, :] + urecv[392:504, :])
        for l in range(1, LEVELS):
            for d in range(1, 2**l):
                at = at8(TOP[l] + lax.rem(flip(a, d), 2**l) * 8)
                push(ubuf.at[pl.ds(at, 8)], lurecv.at[pl.ds(8 * (SLOT[l] + d - 1), 8)], LU + l, flip(a, d), b)

    def form_m0():
        done(recv, AY)
        mbuf[0:16, :] = wcpl[0:16, :] + dot3(split(wcpl[0:16, :]), split(aall[0].reshape(256, 256)))

    def spread(l, value):
        gath[l, pl.ds(own8, 8), :] = value
        mine = gath.at[l, pl.ds(own8, 8)]
        rowpeers(lambda row: push(mine, mine, AG + l, a, row))

    def load_sum(l):
        total = ubuf[pl.ds(at8(TOP[l] + lax.rem(a, 2**l) * 8), 8), :]
        done(recv, LU + l)
        for d in range(1, 2**l):
            total = total + lurecv[8 * (SLOT[l] + d - 1) : 8 * (SLOT[l] + d), :]
        return total

    eye = lax.broadcasted_iota(jnp.int32, (8, 8), 0) == lax.broadcasted_iota(jnp.int32, (8, 8), 1)

    def pivots(l):
        return jnp.sum(jnp.where(eye, jnp.broadcast_to(wpiv[l : l + 1, :], (8, 8)), 0.0), axis=1, keepdims=True)

    def over_leaves(l, sem, rows, first_slot, slots, count):
        for d in range(1, count):
            at = at8(rows + lax.rem(flip(a, d), count) * 8)
            push(part.at[l, pl.ds(at, 8)], slots.at[pl.ds(8 * (first_slot + d - 1), 8)], sem, flip(a, d), b)

    def collect(sem, slots, first_slot, count, total):
        if count > 1:
            done(recv, sem)
            for d in range(1, count):
                total = total + slots[8 * (first_slot + d - 1) : 8 * (first_slot + d), :]
        return total

    def form_m(l):
        n = 2**l
        rows = 2 * n * 8
        done(recv, AY + l)
        own = wcpl[LINK[l] : LINK[l] + rows, :]
        total = own
        for d in range(n):
            if d == 0:
                left = own
            else:
                if l == 2 or d == 1:
                    if not (l == 2 and d == 1):
                        first = 16 if d == 1 else 48
                        done(recv, BX + d)
                at = 96 * (d - 1) + LINK[l] - 16
                left = bpeer[at : at + rows, :]
            block = aall[n - 1 + lax.rem(flip(a, d), n)].reshape(256, 256)
            total = total + dot3(split(left), split(block))
        mbuf[LINK[l] : LINK[l] + rows, :] = total

    def keep_z(l, res, own_part):
        value = collect(YX + l, yrecv, SLOT[l], 2**l, res + own_part)
        value = value / pivots(l)
        at = at8(TOP[l] + lax.rem(a, 2**l) * 8)
        zbuf[pl.ds(at, 8), :] = value
        mine = zbuf.at[pl.ds(at, 8)]
        for d in range(1, 2**l):
            push(mine, mine, ZX + l, flip(a, d), b)
        return value

    below = None
    zs = []
    pending = None
    fetch[7].wait()
    fetch[8].wait()
    for l in range(LEVELS):
        n = 2**l
        if l:
            res = wrhs[l] - load_sum(l) - below
        else:
            done(recv, U0)
            res = wrhs[0] - tree(u0recv)
        spread(l, res)
        if l == 0:
            zpeers(lambda z2, row: push(aall.at[pl.ds(3, 4), b], aall.at[pl.ds(3, 4), b], AZ + 2, a, row))
            place_terms()
            form_m0()
            for q in range(2):
                m0all[q, b] = mbuf[8 * q : 8 * q + 8, :]
        if l == 1:
            done(recv, AZ + 2)
            forward_a(2, 0, 4)
        if l == 2:
            zpeers(lambda z2, row: push(m0all.at[:, b], m0all.at[:, b], MZ, a, row))
        if l == 2:
            z0all[pl.ds(own8, 8), :] = zs[0]
            rowpeers(lambda row: push(z0all.at[pl.ds(own8, 8)], z0all.at[pl.ds(own8, 8)], ZA, a, row))
        if l == 3:
            done(recv, MZ)
            slab0 = m0all.at[:, pl.ds(y * NZ, NZ)]
            ypeers(lambda row: push(slab0, slab0, MY, a, row))
        if l in (1, 2):
            form_m(l)
        if pending is not None:
            zs.append(keep_z(l - 1, *pending))
        lhs = strict[TOP[l] : TOP[l] + 8 * n, :]
        if l < 3:
            lhs = jnp.concatenate([lhs, mbuf[LINK[l] : LINK[l] + 16 * n, :]], axis=0)
        lhs = split(lhs)
        done(recv, AG + l)
        out = dot3(lhs, split(gath[l]))
        part[l, pl.ds(0, out.shape[0]), :] = out
        if l < 3:
            over_leaves(l, PX + l, 8 * n, SLOT[l + 1], precv, 2 * n)
        over_leaves(l, YX + l, 0, SLOT[l], yrecv, n)
        own_y = part[l, pl.ds(at8(lax.rem(a, n) * 8), 8), :]
        if l == 0:
            sum_terms()
        if l < 3:
            below = part[l, pl.ds(at8(8 * n + lax.rem(a, 2 * n) * 8), 8), :]
            below = collect(PX + l, precv, SLOT[l + 1], 2 * n, below)
        pending = (res, own_y)
    zs.append(keep_z(3, *pending))

    def fill(value, first):
        before = [jnp.zeros((first, 128), F32)] if first else []
        after = 128 - first - value.shape[0]
        return split(jnp.concatenate(before + [value] + ([jnp.zeros((after, 128), F32)] if after else []), axis=0))

    def own_half(l):
        n = 2**l
        if l:
            done(recv, ZX + l)
        return dot3(strict_t, fill(zbuf[TOP[l] : TOP[l] + 8 * n, :], TOP[l]))

    def reduce_rows(l, value, total):
        rsend[l] = value
        rrecv[l, pl.ds(own8, 8), :] = rsend[l, pl.ds(own8, 8), :]
        rowpeers(lambda row: push(rsend.at[l, pl.ds(at8(row * 8), 8)], rrecv.at[l, pl.ds(own8, 8)], RS + l, a, row))

    def reduced(l, total):
        done(recv, RS + l)
        return total + tree(rrecv.at[l])

    reduce_rows(3, own_half(3), None)
    m_t = jnp.concatenate([mbuf[0:112, :], jnp.zeros((16, 256), F32)], axis=0)
    m_t = split(jnp.concatenate([m_t[:, :128].T, m_t[:, 128:].T], axis=0))
    done(recv, MY)
    for q in range(4):
        for c in range(2):
            blk = m0all[q // 2, 16 * (q % 2) : 16 * (q % 2) + 16].reshape(128, 256)[:, 128 * c : 128 * c + 128]
            h, lo = split(blk.T)
            m0t_h[128 * c : 128 * c + 128, 128 * q : 128 * q + 128] = h
            m0t_l[128 * c : 128 * c + 128, 128 * q : 128 * q + 128] = lo

    for l in (3, 2, 1):
        n = 2**l
        if l > 1:
            ahead = own_half(l - 1)
        if l == 2:
            done(recv, ZA)
            a0 = aall[0].reshape(256, 256)
            a0 = jnp.concatenate([a0[:, :128].T, a0[:, 128:].T], axis=0)
            c0[...] = z0all[...] + dot3(split(a0), split(z0all[...]))
        if l == 1:
            for m in (2, 3):
                done(recv, PY + m)
            chosen = sel[0:32, 0:32].astype(BF16)
            pieces = []
            for j in range(16):
                ih, i8 = divmod(j, 8)
                pieces.append(jnp.concatenate([xpath[pl.ds(128 * (2 * h + ih) + i8, 16, stride=8), :] for h in range(2)], axis=0))
            pieces = split(jnp.concatenate(pieces, axis=1))
            picked = mm(chosen, pieces[0]) + mm(chosen, pieces[1])
            for j in range(16):
                psend[pl.ds(j, 32, stride=16), :] = picked[:, 128 * j : 128 * j + 128]
            precv2[pl.ds(own64, 64), :] = psend[pl.ds(own64, 64), :]
        value = reduced(l, zs[l])
        if l > 1:
            at = at8(TOP[l] + lax.rem(a, n) * 8)
            xbuf[pl.ds(at, 8), :] = value
            mine = xbuf.at[pl.ds(at, 8)]
            for d in range(1, n):
                push(mine, mine, XX + l, flip(a, d), b)
            out_win[l] = value
            done(recv, XX + l)
            level = xbuf[TOP[l] : TOP[l] + 8 * n, :]
            reduce_rows(l - 1, ahead - dot3(m_t, fill(level, LINK[l - 1])), None)
            block = xbuf.at[pl.ds(TOP[l], 8 * n)]
            there = xpath.at[pl.ds(at8(y * 128 + TOP[l]), 8 * n)]
            ypeers(lambda row: push(block, there, PY + l, a, row))
            xpath[pl.ds(at8(y * 128 + TOP[l]), 8 * n), :] = level
        else:
            half = lax.rem(a, 2)
            x1all[half, b] = value
            rowpeers(lambda row: push(x1all.at[half, b], x1all.at[half, b], X1, a, row))
            zpeers(lambda z2, row: push(psend.at[pl.ds(at8(z2 * 64), 64)], precv2.at[pl.ds(own64, 64)], PICK, a, row))
            out_win[l] = value

    done(recv, X1)
    push(x1all.at[half], x1all.at[half], XS, flip(a, 1), b)
    done(recv, XS)
    x1 = x1all[...].reshape(512, 128)
    x0all[...] = c0[...] - dot3((m0t_h[...], m0t_l[...]), split(x1))
    out_win[0] = x0all[pl.ds(own8, 8), :]
    tiles = [x0all[0:128, :], x0all[128:256, :]] + [x1[128 * q : 128 * q + 128] for q in range(4)]
    done(recv, PICK)
    rows = []
    for t in range(4):
        for i in range(16):
            ih, z2 = divmod(i, 8)
            at = z2 * 64 + t * 16 + ih * 8
            here = precv2[at : at + 8, :]
            for p in range(6):
                here = here + base[t][p] * tiles[p][8 * i : 8 * i + 8]
            rows.append(here)
    got = split(jnp.concatenate(rows, axis=0))
    for r in range(4):
        s = slice(128 * r, 128 * r + 128)
        yloc[s, :] = zloc[s, :] - dot3((ct_h[s, :], ct_l[s, :]), got)
    after = split(yloc[...])
    for r in range(4):
        s = slice(128 * r, 128 * r + 128)
        k = slice(128 * r, 512)
        out_loc[s, :] = yloc[s, :] + dot3((st_h[s, k], st_l[s, k]), (after[0][k], after[1][k]))

    for sem in views:
        done(send, sem)


def shards(loc_rhs, loc_inverse, loc_coupling, loc_pivots, pattern, win_rhs, win_pivots, win_inverse, win_coupling):
    vmem = pl.BlockSpec(memory_space=pltpu.VMEM)
    specs = [pl.BlockSpec(memory_space=pl.ANY)] * 9
    out_loc, out_win = pl.pallas_call(
        kernel,
        out_shape=(jax.ShapeDtypeStruct((512, 128), F32), jax.ShapeDtypeStruct((LEVELS, 8, 128), F32)),
        in_specs=specs,
        out_specs=(vmem, vmem),
        scratch_shapes=[
            pltpu.VMEM((512, 128), F32),
            pltpu.VMEM((512, 512), F32),
            pltpu.VMEM((512, 512), F32),
            pltpu.VMEM((1, 512), F32),
            pltpu.SMEM((1, 4), jnp.int32),
            pltpu.VMEM((LEVELS, 8, 128), F32),
            pltpu.VMEM((LEVELS, 8), F32),
            pltpu.VMEM((120, 256), F32),
            pltpu.VMEM((112, 256), F32),
            pltpu.VMEM((256, 128), F32),
            pltpu.VMEM((256, 128), F32),
            pltpu.VMEM((256, 128), F32),
            pltpu.VMEM((2, NB, 8, 128), F32),
            pltpu.VMEM((256, 128), F32),
            pltpu.VMEM((256, 128), F32),
            pltpu.VMEM((2, NB, 8, 256), F32),
            pltpu.VMEM((256, 512), BF16),
            pltpu.VMEM((256, 512), BF16),
            pltpu.SemaphoreType.DMA((9,)),
            pltpu.VMEM((512, 512), BF16),
            pltpu.VMEM((512, 512), BF16),
            pltpu.VMEM((512, 512), BF16),
            pltpu.VMEM((512, 512), BF16),
            pltpu.VMEM((512, 128), F32),
            pltpu.VMEM((512, 128), F32),
            pltpu.VMEM((8, 4, 128), F32),
            pltpu.VMEM((128, 128), F32),
            pltpu.VMEM((512, 128), F32),
            pltpu.VMEM((512, 128), F32),
            pltpu.VMEM((512, 128), F32),
            pltpu.VMEM((512, 128), F32),
            pltpu.VMEM((128, 128), F32),
            pltpu.VMEM((88, 128), F32),
            pltpu.VMEM((128, 256), F32),
            pltpu.VMEM((7, NB, 8, 256), F32),
            pltpu.VMEM((288, 256), F32),
            pltpu.VMEM((112, 256), F32),
            pltpu.VMEM((LEVELS, 256, 128), F32),
            pltpu.VMEM((LEVELS, 96, 128), F32),
            pltpu.VMEM((88, 128), F32),
            pltpu.VMEM((88, 128), F32),
            pltpu.VMEM((120, 128), F32),
            pltpu.VMEM((120, 128), F32),
            pltpu.VMEM((LEVELS, 256, 128), F32),
            pltpu.VMEM((LEVELS, 256, 128), F32),
            pltpu.VMEM((512, 128), F32),
            pltpu.VMEM((512, 128), F32),
            pltpu.VMEM((512, 128), F32),
            pltpu.SemaphoreType.DMA((NSEM,)),
            pltpu.SemaphoreType.DMA((NSEM,)),
        ],
        compiler_params=pltpu.CompilerParams(collective_id=0, has_side_effects=True),
    )(
        loc_rhs[0, 0], loc_inverse[0, 0], loc_coupling[0, 0], loc_pivots[0], pattern[0],
        win_rhs, win_pivots, win_inverse[0], win_coupling[0],
    )
    return out_loc[None, None], out_win


def solution(mesh):
    return jax.shard_map(
        shards,
        mesh=mesh,
        in_specs=(
            P("leaf", "row", None, None),
            P("leaf", "row", None, None),
            P("leaf", "row", None, None),
            P("leaf", "row", None),
            P("leaf", "row", None),
            P(None, ("leaf", "row"), None),
            P(None, ("leaf", "row")),
            P("row", None, "leaf"),
            P("row", None, "leaf"),
        ),
        out_specs=(P("leaf", "row", None, None), P(None, ("leaf", "row"), None)),
        check_vma=False,
    )
```
